32 devices in a mesh: stream: 4 (over y, x), tile: 8 (over z, core).
Axes of the slice: x: 2, y: 2, z: 4, core: 2. Of those that a mesh axis runs over, the one named last changes fastest.
Arguments:
- concentration: bfloat16 [2, 768, 256, 128], P(None, 'stream', 'tile'), may hold values from 0.29882812 to 3
- potential: bfloat16 [768, 256, 128], P('stream', 'tile'), may hold values from -4 to 4
- diffusivity: bfloat16 [768, 256, 128], P('stream', 'tile'), may hold values from 0.5 to 2
- spacer: int32 [768, 256, 128], P('stream', 'tile'), may hold values 0 or 1
- velocity: bfloat16 [3, 768, 256, 128], P(None, 'stream', 'tile'), may hold values from -4 to 4
- balance_plan: int32 [768, 1], P(('stream', 'tile')), may hold values from 0 to 7; in each aligned block of 24 rows (0 to 23, 24 to 47, ...) at most 6 rows name the same one
Outputs:
- concentration_next: bfloat16 [2, 768, 256, 128], P(None, 'stream', 'tile')
- velocity_next: bfloat16 [3, 768, 256, 128], P(None, 'stream', 'tile')
- owned_charge: bfloat16 [1536, 32, 1024], P(('stream', 'tile'))
The draws below stay inside these ranges and needn't reach their ends.
Inputs may be any that keep to these rules, and one draw needn't show every extreme that they name: 1 marks fluid, 0 a spacer filament. `balance_plan`: the 24 blocks of one slab tile (aligned rows of one device) name owners among the 8 tiles of the same slab; at most 6 of them name the same owner, and some slab tile has exactly 6 with one owner.
All inputs are finite; a program needn't handle non-finite values. No bound on the sum of `spacer` on one device may be relied on, other than what follows from the above.
Results may differ from the reference program's by a relative error of at most 0.011.
Values may be sent and summed in bfloat16 or wider, within the bound.
No kernel may reach another device: no remote copies, remote signals or barrier semaphores. Data moves between devices by JAX's collectives and lax.ppermute only.
A program may use at most 256 MiB of HBM per device.

```python
import math
import jax
import jax.numpy as jnp
import numpy as np
from jax import lax

BLK = 32
BX = 6
BZ = 4
BPD = 24
CAP = 6
SLOTS = 48
NX = 768
NY = 256
NZ = 128
N_STREAM = 4
N_TILE = 8


def with_ends(array, stream_key, low, largest):
    index_at = [jax.random.randint(jax.random.fold_in(stream_key, axis), (), 0, length) for axis, length in enumerate(array.shape)]
    main_axis = array.shape.index(max(array.shape))
    neighbour = index_at[:main_axis] + [(index_at[main_axis] + 1) % array.shape[main_axis]] + index_at[main_axis + 1:]
    return array.at[tuple(index_at)].set(low).at[tuple(neighbour)].set(largest)


def block_scale(rng, dims, cuts, smallest, largest):
    factor_of, own = 1.0, jax.random.fold_in(rng, 6)
    for dim, shards_of in cuts:
        draws = jnp.exp(jax.random.uniform(jax.random.fold_in(own, dim), (shards_of,), jnp.float32, smallest / len(cuts), largest / len(cuts)))
        factor_of = factor_of * jnp.repeat(draws, dims[dim] // shards_of).reshape([-1 if axis == dim else 1 for axis in range(len(dims))])
    return factor_of


def shared_out(own_key, own, number, rows, number_of, top, reach, skew):
    sequence = jax.random.permutation(own_key, number_of)
    packed, usual = shares(number_of, rows * top, reach, skew, True), shares(number_of, rows * top, reach, skew, False)
    places = jnp.arange(number_of)

    def named(tallies, turn):
        used = int((tallies > 0).sum())
        fixed = max(1, used // 4)
        shifted = fixed + (places - fixed + turn * (used - fixed)) % max(1, number_of - fixed)
        return jnp.zeros((number_of,), jnp.int32).at[sequence[jnp.where(places < fixed, places, shifted)]].set(jnp.asarray(tallies, jnp.int32))

    tallies = jnp.where(number % 4 == 0, named(packed, number // 4), named(usual, number - number // 4 - 1))
    mixed = jax.random.permutation(jax.random.fold_in(own, 3), number_of)
    source_of, sink = mixed[0:number_of // 2 * 2:2], mixed[1:number_of // 2 * 2:2]
    margin = jnp.minimum(tallies[source_of] - 1, reach - tallies[sink]) // 2
    margin = jnp.where((source_of == sequence[0]) | (sink == sequence[0]) | (tallies[sink] == 0), 0, jnp.maximum(margin, 0))
    shifted = jax.random.randint(jax.random.fold_in(own, 4), (number_of // 2,), 0, 1 << 20) % (margin + 1)
    tallies = tallies.at[source_of].add(-shifted).at[sink].add(shifted)
    members = jnp.searchsorted(jnp.cumsum(tallies), jnp.arange(rows * top), side="right").astype(jnp.int32)
    listing = members.reshape(top, rows).T
    listing = listing[jax.random.permutation(jax.random.fold_in(own, 1), rows)]
    turn = jax.random.randint(jax.random.fold_in(own, 2), (rows, 1), 0, top)
    return jnp.take_along_axis(listing, (jnp.arange(top)[None, :] + turn) % top, axis=1)


def shares(amount, total, reach, slope, full):
    loads = [(1 << 20) // math.isqrt(grade ** slope) + 1 for grade in range(1, amount + 1)]
    largest = reach if full else min(reach, max(-(-total // amount), total * loads[0] // sum(loads)))
    least = 1 if total - largest >= amount - 1 else 0
    given, spare = [largest] + [least] * (amount - 1), total - largest - least * (amount - 1)
    while spare > 0:
        free = [i for i in range(1, amount) if given[i] < largest] or [i for i in range(1, amount) if given[i] < reach]
        pool, remaining = sum([loads[i] for i in free]), spare
        for i in free:
            extra = min(reach - given[i], max(1, remaining * loads[i] // pool), spare)
            given[i] = given[i] + extra
            spare = spare - extra
    return np.array(given)


def normal_values(stream_key, extent, width, most, shards=(), kind=jnp.bfloat16):
    values = width * jax.random.normal(stream_key, extent, jnp.float32)
    if shards:
        values = values * block_scale(stream_key, extent, shards, -0.22, 0.18)
    return jnp.clip(values, -most, most).astype(kind)


def setup_inputs(seed: int = 0) -> dict:
    seeds = jax.random.split(jax.random.key(seed), 7)
    concentration = jnp.clip(jnp.exp(math.log(3.0) - 2.306499 * jax.random.uniform(seeds[0], (2, NX, NY, NZ), jnp.float32) ** block_scale(seeds[0], (2, NX, NY, NZ), ((1, 4), (2, 8)), -0.2, 0.2)), 0.29882812, 3.0).astype(jnp.bfloat16)
    potential = normal_values(seeds[1], (NX, NY, NZ), 1.0, 4.0, ((0, 4), (1, 8)))
    diffusivity = jnp.clip(jnp.exp(math.log(2.0) - 1.3862944 * jax.random.uniform(seeds[2], (NX, NY, NZ), jnp.float32) ** block_scale(seeds[2], (NX, NY, NZ), ((0, 4), (1, 8)), -0.2, 0.2)), 0.5, 2.0).astype(jnp.bfloat16)
    spacer = with_ends((jax.random.randint(seeds[3], (NX, NY, NZ), 0, 4) < 3).astype(jnp.int32), jax.random.fold_in(seeds[3], 1), 0, 1)
    velocity = normal_values(seeds[4], (3, NX, NY, NZ), 1.0, 4.0, ((1, 4), (2, 8)))
    balance_plan_keys = jax.random.split(jax.random.fold_in(seeds[5], 1), (N_STREAM * N_TILE * BPD) // BPD)
    balance_plan_turns = jax.random.permutation(jax.random.fold_in(seeds[5], 3), (N_STREAM * N_TILE * BPD) // BPD)
    balance_plan = jax.vmap(lambda own, number: shared_out(jax.random.fold_in(seeds[5], 2), own, number, BPD, N_TILE, 1, CAP, 1))(balance_plan_keys, balance_plan_turns).reshape((N_STREAM * N_TILE * BPD, 1))
    return dict(concentration=concentration, potential=potential, diffusivity=diffusivity, spacer=spacer, velocity=velocity, balance_plan=balance_plan)


ion_step = 0.04
flow_step = 0.1
viscosity = 0.5
species_diff = (1.0, 1.5)
species_charge = (1.0, -1.0)

def neighbor_view(source, axis_number, offset):
    first = [1, 1, 1]
    first[axis_number] = 1 + offset
    return source[first[0]:first[0] + source.shape[0] - 2, first[1]:first[1] + source.shape[1] - 2, first[2]:first[2] + source.shape[2] - 2]

def interior_view(source):
    return source[1:-1, 1:-1, 1:-1]

def ion_update(padded):
    fields = padded.astype(jnp.float32)
    electric = fields[2]
    openness = fields[3]
    open_mid = interior_view(openness)
    pot_mid = interior_view(electric)
    updated = []
    for species in range(2):
        density = fields[species]
        dens_mid = interior_view(density)
        running = jnp.zeros_like(dens_mid)
        for axis_number in range(3):
            for offset in (-1, 1):
                dens_near = neighbor_view(density, axis_number, offset)
                pot_near = neighbor_view(electric, axis_number, offset)
                face_coef = jnp.sqrt(open_mid * neighbor_view(openness, axis_number, offset))
                running = running + face_coef * (dens_near - dens_mid + species_charge[species] * 0.5 * (dens_mid + dens_near) * (pot_near - pot_mid))
        updated.append(dens_mid + ion_step * species_diff[species] * running)
    return jnp.stack(updated)

def flow_update(flow_pad, pot_pad, charge, fluid_cells):
    flow_field = flow_pad.astype(jnp.float32)
    electric = pot_pad.astype(jnp.float32)
    middle = [interior_view(flow_field[component]) for component in range(3)]
    result = []
    for component in range(3):
        advect = jnp.zeros_like(middle[component])
        diffuse = -6.0 * middle[component]
        for axis_number in range(3):
            forward = neighbor_view(flow_field[component], axis_number, 1)
            backward = neighbor_view(flow_field[component], axis_number, -1)
            advect = advect + middle[axis_number] * 0.5 * (forward - backward)
            diffuse = diffuse + forward + backward
        field_part = -0.5 * (neighbor_view(electric, component, 1) - neighbor_view(electric, component, -1))
        result.append(fluid_cells * (middle[component] + flow_step * (viscosity * diffuse - advect + charge * field_part)))
    return jnp.stack(result).astype(jnp.bfloat16)

def wrap_pad(stack):
    stack = jnp.concatenate([stack[:, :, -1:], stack, stack[:, :, :1]], axis=2)
    return jnp.pad(stack, ((0, 0), (0, 0), (0, 0), (1, 1)))

def reference(concentration, potential, diffusivity, spacer, velocity, balance_plan):
    openness = jnp.where(spacer > 0, diffusivity, jnp.zeros_like(diffusivity))
    moving = jnp.where(spacer[None] > 0, velocity, jnp.zeros_like(velocity))
    slab_count = NX // BLK

    def one_slab(number):
        positions = (number * BLK - 1 + jnp.arange(BLK + 2, dtype=jnp.int32)) % NX
        ions = jnp.concatenate([jnp.take(concentration, positions, axis=1), jnp.take(potential, positions, axis=0)[None], jnp.take(openness, positions, axis=0)[None]], axis=0)
        ions = wrap_pad(ions)
        motion = wrap_pad(jnp.take(moving, positions, axis=1))
        conc_new = ion_update(ions).astype(jnp.bfloat16)
        charge = conc_new[0].astype(jnp.float32) - conc_new[1].astype(jnp.float32)
        fluid_cells = (lax.dynamic_slice_in_dim(spacer, number * BLK, BLK, 0) > 0).astype(jnp.float32)
        flow_new = flow_update(motion, ions[2], charge, fluid_cells)
        return (conc_new, charge.astype(jnp.bfloat16), flow_new)
    conc_slabs, charge_slabs, flow_slabs = lax.map(one_slab, jnp.arange(slab_count, dtype=jnp.int32))
    conc_out = conc_slabs.transpose(1, 0, 2, 3, 4).reshape(2, NX, NY, NZ)
    flow_out = flow_slabs.transpose(1, 0, 2, 3, 4).reshape(3, NX, NY, NZ)
    charge_field = charge_slabs.reshape(NX, NY, NZ)
    blocks = charge_field.reshape(N_STREAM, BX, BLK, N_TILE, BLK, BZ, BLK).transpose(0, 3, 1, 5, 2, 4, 6).reshape(N_STREAM, N_TILE, BPD, BLK, BLK * BLK)
    owners = balance_plan[:, 0].reshape(N_STREAM, N_TILE, BPD)
    same_owner = owners[:, :, :, None] == owners[:, :, None, :]
    earlier = jnp.arange(BPD, dtype=jnp.int32)[:, None] < jnp.arange(BPD, dtype=jnp.int32)[None, :]
    ranking = lax.optimization_barrier(jnp.sum(jnp.logical_and(same_owner, earlier[None, None]).astype(jnp.int32), axis=2)).astype(jnp.int32)
    slot_index = jnp.arange(N_TILE, dtype=jnp.int32)[None, :, None] * CAP + ranking
    stream_index = jnp.broadcast_to(jnp.arange(N_STREAM, dtype=jnp.int32)[:, None, None], owners.shape)
    owned = jnp.zeros((N_STREAM, N_TILE, SLOTS, BLK, BLK * BLK), jnp.bfloat16).at[stream_index, owners, slot_index].set(blocks)
    return (conc_out, flow_out, owned.reshape(N_STREAM * N_TILE * SLOTS, BLK, BLK * BLK))
```

```python
import functools

import jax
import jax.numpy as jnp
from jax import lax
from jax.experimental import pallas as pl
from jax.experimental.pallas import tpu as pltpu
from jax.sharding import PartitionSpec as P

BLK = 32
GRP = 16
TOP = 8
ROWS = 48

ion_step = 0.04
flow_step = 0.1
viscosity = 0.5
species_diff = (1.0, 1.5)

F32 = jnp.float32
BF16 = jnp.bfloat16


def rings(axis):
    count = lax.axis_size(axis)
    forward = [(i, (i + 1) % count) for i in range(count)]
    backward = [(target, source) for source, target in forward]
    return forward, backward


def edges(stack):
    x_fwd, x_bwd = rings("stream")
    y_fwd, y_bwd = rings("tile")
    return (
        lax.ppermute(stack(-1, None), "stream", x_fwd),
        lax.ppermute(stack(0, None), "stream", x_bwd),
        lax.ppermute(stack(None, -1), "tile", y_fwd),
        lax.ppermute(stack(None, 0), "tile", y_bwd),
    )


def pick(array, x, y):
    if x is not None:
        return array[..., x, :, :]
    return array[..., y, :]


def roll_lanes(value, shift):
    return pltpu.roll(value, shift % value.shape[-1], axis=value.ndim - 1)


def face(low, high):
    f = low[3] * high[3]
    h = f * (high[2] - low[2])
    a = f + h
    b = f - h
    return a * high[0] - b * low[0], b * high[1] - a * low[1]


def ion_kernel(
    capacity,
    plan,
    c_hbm,
    p_hbm,
    d_hbm,
    s_hbm,
    xl_hbm,
    xh_hbm,
    yl_hbm,
    yh_hbm,
    cn_hbm,
    out_hbm,
    c_v,
    p_v,
    d_v,
    s_v,
    xl_v,
    xh_v,
    yl_v,
    yh_v,
    yl_f,
    yh_f,
    fld,
    cn_v,
    chs,
    blk,
    zero,
    perm,
    lanes,
    tally,
    in_sem,
    halo_sem,
    cn_sem,
    blk_sem,
    zero_sem,
):
    nx, nz = p_hbm.shape[0], p_hbm.shape[2]
    chunks = nx // BLK
    bz = nz // BLK
    slots = out_hbm.shape[0]
    tiles = slots // capacity
    count = chunks * bz

    def loads(i):
        part = pl.ds(i * BLK, BLK)
        return (
            pltpu.make_async_copy(c_hbm.at[:, part], c_v.at[:, part], in_sem.at[0, i]),
            pltpu.make_async_copy(p_hbm.at[part], p_v.at[part], in_sem.at[1, i]),
            pltpu.make_async_copy(d_hbm.at[part], d_v.at[part], in_sem.at[2, i]),
            pltpu.make_async_copy(s_hbm.at[part], s_v.at[part], in_sem.at[3, i]),
        )

    halos = (
        pltpu.make_async_copy(xl_hbm, xl_v, halo_sem.at[0]),
        pltpu.make_async_copy(xh_hbm, xh_v, halo_sem.at[1]),
        pltpu.make_async_copy(yl_hbm, yl_v, halo_sem.at[2]),
        pltpu.make_async_copy(yh_hbm, yh_v, halo_sem.at[3]),
    )
    for copy in halos:
        copy.start()
    for i in range(chunks):
        for copy in loads(i):
            copy.start()

    zero[...] = jnp.zeros_like(zero)
    width = BLK * GRP
    r = lax.broadcasted_iota(jnp.int32, (width, width), 0)
    c = lax.broadcasted_iota(jnp.int32, (width, width), 1)
    hit = (r // GRP == c % BLK) & (r % GRP == c // BLK)
    perm[...] = jnp.where(hit, 1.0, 0.0).astype(BF16)
    wide = bz * nz
    r = lax.broadcasted_iota(jnp.int32, (wide, wide), 0)
    c = lax.broadcasted_iota(jnp.int32, (wide, wide), 1)
    hit = (r // nz == (c % nz) // BLK) & (r % nz == (c // nz) * BLK + c % BLK)
    lanes[...] = jnp.where(hit, 1.0, 0.0).astype(BF16)

    @pl.loop(0, tiles)
    def _(o):
        tally[count + o] = 0

    @pl.loop(0, count)
    def _(b):
        o = plan[b]
        rank = tally[count + o]
        tally[b] = o * capacity + rank
        tally[count + o] = rank + 1

    def blank(slot):
        return pltpu.make_async_copy(zero, out_hbm.at[slot], zero_sem.at[slot])

    @pl.loop(0, tiles)
    def _(o):
        @pl.loop(tally[count + o], capacity)
        def _(k):
            blank(o * capacity + k).start()

    for copy in halos:
        copy.wait()
    body = pl.ds(TOP, BLK)

    def root(o):
        return o * lax.rsqrt(jnp.maximum(o, 0.25))

    for plane, ref in ((0, xl_v), (nx + 1, xh_v)):
        for f in range(4):
            v = ref[f].astype(F32)
            v = v * 0.5 if f == 2 else (root(v) if f == 3 else v)
            fld[f, plane, body, :] = v
    for ref, dst in ((yl_v, yl_f), (yh_v, yh_f)):
        for f in range(4):
            v = ref[f].astype(F32)
            v = v * 0.5 if f == 2 else (root(v) if f == 3 else v)
            dst[f] = v

    def prepare(i):
        for copy in loads(i):
            copy.wait()

        @pl.loop(0, BLK)
        def _(q):
            x = i * BLK + q
            fld[0, x + 1, body, :] = c_v[0, x].astype(F32)
            fld[1, x + 1, body, :] = c_v[1, x].astype(F32)
            fld[2, x + 1, body, :] = p_v[x].astype(F32) * 0.5
            d = d_v[x].astype(F32)
            fld[3, x + 1, body, :] = jnp.where(s_v[x] > 0, d * lax.rsqrt(d), 0.0)
            for f in range(4):
                fld[f, x + 1, pl.ds(TOP - 1, 1), :] = yl_f[f, pl.ds(x, 1), :]
                fld[f, x + 1, pl.ds(TOP + BLK, 1), :] = yh_f[f, pl.ds(x, 1), :]

    def plane_of(x, rows):
        return [fld[f, x, rows, :] for f in range(4)]

    first_lane = lax.broadcasted_iota(jnp.int32, (BLK, nz), 1) == 0

    def update(i, carry):
        def step(q, carry):
            x = i * BLK + q
            mid = plane_of(x + 1, body)
            fx = face(mid, plane_of(x + 2, body))
            fy = face(
                plane_of(x + 1, pl.ds(TOP - 1, BLK + 8)), plane_of(x + 1, pl.ds(TOP, BLK + 8))
            )
            below = [roll_lanes(v, 1) for v in mid]
            below[3] = jnp.where(first_lane, 0.0, below[3])
            fz = face(below, mid)
            new = []
            for s in range(2):
                total = (fx[s] - carry[s]) + (fy[s][1 : BLK + 1] - fy[s][:BLK])
                total = total + (roll_lanes(fz[s], -1) - fz[s])
                new.append((mid[s] + (ion_step * species_diff[s]) * total).astype(BF16))
                cn_v[s, x] = new[s]
            charge = new[0].astype(F32) - new[1].astype(F32)
            chs[pl.ds(pl.multiple_of(q * BLK, BLK), BLK), :] = charge.astype(BF16)
            return fx

        return lax.fori_loop(0, BLK, step, carry)

    def saves(i):
        part = pl.ds(i * BLK, BLK)
        return pltpu.make_async_copy(cn_v.at[:, part], cn_hbm.at[:, part], cn_sem.at[i])

    def put(b):
        return pltpu.make_async_copy(blk.at[b], out_hbm.at[tally[b]], blk_sem.at[b])

    prepare(0)
    start = face(plane_of(0, body), plane_of(1, body))

    def chunk(i, carry):
        @pl.when(i + 1 < chunks)
        def _():
            prepare(i + 1)

        carry = update(i, carry)
        saves(i).start()
        for g in range(BLK // GRP):
            t = jnp.dot(perm[...], chs[g * width : (g + 1) * width, :], preferred_element_type=F32)
            t = t.astype(BF16)
            wideset = jnp.concatenate(
                [
                    jnp.concatenate(
                        [t[(j * bz + m) * GRP : (j * bz + m + 1) * GRP] for m in range(bz)], axis=1
                    )
                    for j in range(BLK // bz)
                ],
                axis=0,
            )
            res = jnp.dot(wideset, lanes[...], preferred_element_type=F32).astype(BF16)
            for k in range(bz):
                for j in range(BLK // bz):
                    blk[i * bz + k, g * GRP : (g + 1) * GRP, j * nz : (j + 1) * nz] = res[
                        j * GRP : (j + 1) * GRP, k * nz : (k + 1) * nz
                    ]
        for k in range(bz):
            put(i * bz + k).start()
        return carry

    lax.fori_loop(0, chunks, chunk, start)

    @pl.loop(0, chunks)
    def _(i):
        saves(i).wait()

    @pl.loop(0, count)
    def _(b):
        put(b).wait()

    @pl.loop(0, tiles)
    def _(o):
        @pl.loop(tally[count + o], capacity)
        def _(k):
            blank(o * capacity + k).wait()


def ion_call(plan, c, p, d, s, halo, capacity, tiles):
    _, nx, ny, nz = c.shape
    count = plan.shape[0]
    chunks = nx // BLK
    bz = nz // BLK
    anywhere = pl.BlockSpec(memory_space=pl.ANY)
    vm = pltpu.VMEM
    dma = pltpu.SemaphoreType.DMA
    return pl.pallas_call(
        functools.partial(ion_kernel, capacity),
        name="ion",
        out_shape=(
            jax.ShapeDtypeStruct(c.shape, BF16),
            jax.ShapeDtypeStruct((tiles * capacity, BLK, BLK * BLK), BF16),
        ),
        in_specs=[pl.BlockSpec(memory_space=pltpu.SMEM)] + [anywhere] * 8,
        out_specs=(anywhere, anywhere),
        scratch_shapes=[
            vm(c.shape, BF16),
            vm(p.shape, BF16),
            vm(d.shape, BF16),
            vm(s.shape, jnp.int32),
            vm((4, ny, nz), BF16),
            vm((4, ny, nz), BF16),
            vm((4, nx, nz), BF16),
            vm((4, nx, nz), BF16),
            vm((4, nx, nz), F32),
            vm((4, nx, nz), F32),
            vm((4, nx + 2, ROWS, nz), F32),
            vm(c.shape, BF16),
            vm((BLK * BLK, nz), BF16),
            vm((count, BLK, BLK * BLK), BF16),
            vm((BLK, BLK * BLK), BF16),
            vm((BLK * GRP, BLK * GRP), BF16),
            vm((bz * nz, bz * nz), BF16),
            pltpu.SMEM((count + tiles,), jnp.int32),
            dma((4, chunks)),
            dma((4,)),
            dma((chunks,)),
            dma((count,)),
            dma((tiles * capacity,)),
        ],
        compiler_params=pltpu.CompilerParams(vmem_limit_bytes=52 * 2**20),
        cost_estimate=pl.CostEstimate(
            flops=60 * p.size, bytes_accessed=20 * p.size, transcendentals=p.size
        ),
    )(plan, c, p, d, s, *halo)


def flow_kernel(
    u_hbm,
    p_hbm,
    s_hbm,
    cn_hbm,
    uxl_hbm,
    uxh_hbm,
    uyl_hbm,
    uyh_hbm,
    pxl_hbm,
    pxh_hbm,
    pyl_hbm,
    pyh_hbm,
    un_hbm,
    u_v,
    p_v,
    s_v,
    cn_v,
    uxl_v,
    uxh_v,
    uyl_v,
    uyh_v,
    pxl_v,
    pxh_v,
    pyl_v,
    pyh_v,
    yl_f,
    yh_f,
    fld,
    un_v,
    in_sem,
    halo_sem,
    un_sem,
):
    nx, nz = p_hbm.shape[0], p_hbm.shape[2]
    chunks = nx // BLK

    def loads(i):
        part = pl.ds(i * BLK, BLK)
        return (
            pltpu.make_async_copy(u_hbm.at[:, part], u_v.at[:, part], in_sem.at[0, i]),
            pltpu.make_async_copy(p_hbm.at[part], p_v.at[part], in_sem.at[1, i]),
            pltpu.make_async_copy(s_hbm.at[part], s_v.at[part], in_sem.at[2, i]),
            pltpu.make_async_copy(cn_hbm.at[:, part], cn_v.at[:, part], in_sem.at[3, i]),
        )

    pairs = (
        (uxl_hbm, uxl_v),
        (uxh_hbm, uxh_v),
        (uyl_hbm, uyl_v),
        (uyh_hbm, uyh_v),
        (pxl_hbm, pxl_v),
        (pxh_hbm, pxh_v),
        (pyl_hbm, pyl_v),
        (pyh_hbm, pyh_v),
    )
    halos = [
        pltpu.make_async_copy(src.at[2] if n > 3 else src, dst, halo_sem.at[n])
        for n, (src, dst) in enumerate(pairs)
    ]
    for copy in halos:
        copy.start()
    for i in range(chunks):
        for copy in loads(i):
            copy.start()
    for copy in halos:
        copy.wait()
    body = pl.ds(TOP, BLK)
    for plane, ref, pref in ((0, uxl_v, pxl_v), (nx + 1, uxh_v, pxh_v)):
        for f in range(3):
            fld[f, plane, body, :] = ref[f].astype(F32)
        fld[3, plane, body, :] = pref[...].astype(F32)
    for ref, pref, dst in ((uyl_v, pyl_v, yl_f), (uyh_v, pyh_v, yh_f)):
        for f in range(3):
            dst[f] = ref[f].astype(F32)
        dst[3] = pref[...].astype(F32)

    def prepare(i):
        for copy in loads(i):
            copy.wait()

        @pl.loop(0, BLK)
        def _(q):
            x = i * BLK + q
            fluid = s_v[x] > 0
            for f in range(3):
                fld[f, x + 1, body, :] = jnp.where(fluid, u_v[f, x].astype(F32), 0.0)
            fld[3, x + 1, body, :] = p_v[x].astype(F32)
            for f in range(4):
                fld[f, x + 1, pl.ds(TOP - 1, 1), :] = yl_f[f, pl.ds(x, 1), :]
                fld[f, x + 1, pl.ds(TOP + BLK, 1), :] = yh_f[f, pl.ds(x, 1), :]

    half = 16
    lane = lax.broadcasted_iota(jnp.int32, (half, nz), 1)
    first_lane = lane == 0
    last_lane = lane == nz - 1
    k_mid = flow_step * viscosity
    k_adv = flow_step * 0.5

    def below(v):
        return jnp.where(first_lane, 0.0, roll_lanes(v, 1))

    def above(v):
        return jnp.where(last_lane, 0.0, roll_lanes(v, -1))

    def update(i):
        @pl.loop(0, BLK)
        def _(q):
            x = i * BLK + q
            for y0 in range(0, BLK, half):
                at = pl.ds(TOP + y0, half)
                mid = [fld[f, x + 1, at, :] for f in range(3)]
                field = fld[3, x + 1, at, :]
                fluid = s_v[x, pl.ds(y0, half), :] > 0
                cn0 = cn_v[0, x, pl.ds(y0, half), :].astype(F32)
                cn1 = cn_v[1, x, pl.ds(y0, half), :].astype(F32)
                push = (cn0 - cn1) * k_adv
                plus = [k_mid - k_adv * u for u in mid]
                minus = [k_mid + k_adv * u for u in mid]
                for a in range(3):
                    total = mid[a] * (1.0 - 6.0 * k_mid)
                    total = total + fld[a, x + 2, at, :] * plus[0] + fld[a, x, at, :] * minus[0]
                    total = total + fld[a, x + 1, pl.ds(TOP + 1 + y0, half), :] * plus[1]
                    total = total + fld[a, x + 1, pl.ds(TOP - 1 + y0, half), :] * minus[1]
                    total = total + above(mid[a]) * plus[2] + below(mid[a]) * minus[2]
                    if a == 0:
                        rise = fld[3, x + 2, at, :] - fld[3, x, at, :]
                    elif a == 1:
                        rise = (
                            fld[3, x + 1, pl.ds(TOP + 1 + y0, half), :]
                            - fld[3, x + 1, pl.ds(TOP - 1 + y0, half), :]
                        )
                    else:
                        rise = above(field) - below(field)
                    total = jnp.where(fluid, total - push * rise, 0.0)
                    un_v[a, x, pl.ds(y0, half), :] = total.astype(BF16)

    def saves(i):
        part = pl.ds(i * BLK, BLK)
        return pltpu.make_async_copy(un_v.at[:, part], un_hbm.at[:, part], un_sem.at[i])

    prepare(0)

    @pl.loop(0, chunks)
    def _(i):
        @pl.when(i + 1 < chunks)
        def _():
            prepare(i + 1)

        update(i)
        saves(i).start()

    @pl.loop(0, chunks)
    def _(i):
        saves(i).wait()


def flow_call(u, p, s, cn, uhalo, halo):
    _, nx, ny, nz = u.shape
    chunks = nx // BLK
    anywhere = pl.BlockSpec(memory_space=pl.ANY)
    vm = pltpu.VMEM
    dma = pltpu.SemaphoreType.DMA
    return pl.pallas_call(
        flow_kernel,
        name="flow",
        out_shape=jax.ShapeDtypeStruct(u.shape, BF16),
        in_specs=[anywhere] * 12,
        out_specs=anywhere,
        scratch_shapes=[
            vm(u.shape, BF16),
            vm(p.shape, BF16),
            vm(s.shape, jnp.int32),
            vm(cn.shape, BF16),
            vm((3, ny, nz), BF16),
            vm((3, ny, nz), BF16),
            vm((3, nx, nz), BF16),
            vm((3, nx, nz), BF16),
            vm((ny, nz), BF16),
            vm((ny, nz), BF16),
            vm((nx, nz), BF16),
            vm((nx, nz), BF16),
            vm((4, nx, nz), F32),
            vm((4, nx, nz), F32),
            vm((4, nx + 2, ROWS, nz), F32),
            vm(u.shape, BF16),
            dma((4, chunks)),
            dma((8,)),
            dma((chunks,)),
        ],
        compiler_params=pltpu.CompilerParams(vmem_limit_bytes=52 * 2**20),
        cost_estimate=pl.CostEstimate(
            flops=80 * p.size, bytes_accessed=20 * p.size, transcendentals=0
        ),
    )(u, p, s, cn, *uhalo, *halo)


def per_device(concentration, potential, diffusivity, spacer, velocity, balance_plan):
    tiles = lax.axis_size("tile")
    count = balance_plan.shape[0]
    capacity = max(2, (2 * count + tiles - 1) // tiles)
    slots = tiles * capacity

    def ions(x, y):
        solid = pick(spacer, x, y) > 0
        openness = pick(diffusivity, x, y)
        openness = jnp.where(solid, openness, jnp.zeros_like(openness))
        rest = jnp.stack([pick(potential, x, y), openness])
        return jnp.concatenate([pick(concentration, x, y), rest], axis=0)

    def motion(x, y):
        moving = pick(velocity, x, y)
        return jnp.where(pick(spacer, x, y)[None] > 0, moving, jnp.zeros_like(moving))

    halo = edges(ions)
    uhalo = edges(motion)
    conc_next, outgoing = ion_call(
        balance_plan[:, 0], concentration, potential, diffusivity, spacer, halo, capacity, tiles
    )
    outgoing = outgoing.reshape(tiles, capacity, BLK, BLK * BLK)
    owned = lax.all_to_all(outgoing, "tile", split_axis=0, concat_axis=0, tiled=True)
    flow_next = flow_call(velocity, potential, spacer, conc_next, uhalo, halo)
    return conc_next, flow_next, owned.reshape(slots, BLK, BLK * BLK)


def solution(mesh):
    placed = (
        P(None, "stream", "tile", None),
        P("stream", "tile", None),
        P("stream", "tile", None),
        P("stream", "tile", None),
        P(None, "stream", "tile", None),
        P(("stream", "tile"), None),
    )
    return jax.shard_map(
        per_device,
        mesh=mesh,
        in_specs=placed,
        out_specs=(
            P(None, "stream", "tile", None),
            P(None, "stream", "tile", None),
            P(("stream", "tile"), None, None),
        ),
        check_vma=False,
    )
```

```python
import functools

import jax
import jax.numpy as jnp
from jax import lax
from jax.experimental import pallas as pl
from jax.experimental.pallas import tpu as pltpu
from jax.sharding import PartitionSpec as P


BLK = 32
TOP = 8
ROWS = 48

ion_step = 0.04
flow_step = 0.1
viscosity = 0.5
species_diff = (1.0, 1.5)

F32 = jnp.float32
BF16 = jnp.bfloat16

HBM = pl.BlockSpec(memory_space=pltpu.HBM)
PARAMS = pltpu.CompilerParams(vmem_limit_bytes=60 * 2**20)


def rings(axis):
    count = lax.axis_size(axis)
    forward = [(i, (i + 1) % count) for i in range(count)]
    backward = [(target, source) for source, target in forward]
    return forward, backward


def edge_kernel(*refs):
    c_hbm, p_hbm, d_hbm, s_hbm, u_hbm, xf, xl, yf, yl = refs[:9]
    c_x, p_x, d_x, s_x, u_x, c_y, p_y, d_y, s_y, u_y, tmp, tmp_s, x_sem, y_sem = refs[9:]
    nx, ny, nz = p_hbm.shape
    cuts = y_sem.shape[2]
    step = nx // cuts
    sources = (c_hbm, p_hbm, d_hbm, s_hbm, u_hbm)

    def planes(n):
        at = 0 if n == 0 else nx - 1
        copies = []
        for j, (src, dst) in enumerate(zip(sources, (c_x, p_x, d_x, s_x, u_x))):
            part = src.at[:, at] if len(src.shape) == 4 else src.at[at]
            copies.append(pltpu.make_async_copy(part, dst.at[n], x_sem.at[n, j]))
        return copies

    def rows(n, i):
        part = pl.ds(i * step, step)
        row = pl.ds(0 if n == 0 else ny - TOP, TOP)
        copies = []
        for j, (src, dst) in enumerate(zip(sources, (c_y, p_y, d_y, s_y, u_y))):
            if len(src.shape) == 4:
                pair = src.at[:, part, row], dst.at[n, :, part]
            else:
                pair = src.at[part, row], dst.at[n, part]
            copies.append(pltpu.make_async_copy(*pair, y_sem.at[n, j, i]))
        return copies

    for i in range(cuts):
        for n in range(2):
            for copy in rows(n, i):
                copy.start()
    for n in range(2):
        for copy in planes(n):
            copy.start()
    for n, out in enumerate((xf, xl)):
        for copy in planes(n):
            copy.wait()
        solid = s_x[n] > 0
        out[0] = c_x[n, 0]
        out[1] = c_x[n, 1]
        out[2] = p_x[n]
        out[3] = jnp.where(solid, d_x[n].astype(F32), 0.0).astype(BF16)
        for f in range(3):
            out[4 + f] = jnp.where(solid, u_x[n, f].astype(F32), 0.0).astype(BF16)
    size = 16
    for i in range(cuts):
        for n, out in enumerate((yf, yl)):
            for copy in rows(n, i):
                copy.wait()
            row = 0 if n == 0 else TOP - 1

            @pl.loop(0, step // size)
            def _(q, i=i, n=n, out=out, row=row):
                at = pl.ds(pl.multiple_of(i * step + q * size, size), size)
                picked = pl.ds(row, size, stride=TOP)
                tmp_s[...] = s_y[n, at].reshape(size * TOP, nz)
                solid = tmp_s[picked, :] > 0
                loaded = [c_y[n, 0, at], c_y[n, 1, at], p_y[n, at], d_y[n, at]]
                loaded += [u_y[n, f, at] for f in range(3)]
                for f, v in enumerate(loaded):
                    tmp[f] = v.astype(F32).reshape(size * TOP, nz)
                for f in range(7):
                    v = tmp[f, picked, :]
                    if f > 2:
                        v = jnp.where(solid, v, 0.0)
                    out[f, at, :] = v.astype(BF16)


def edges(c, p, d, s, u):
    nx, ny, nz = p.shape
    vm = pltpu.VMEM
    vmem = pl.BlockSpec(memory_space=vm)
    cuts = 4

    def pieces(shape):
        return [
            vm((2,) + (2,) * two + (3,) * three + shape, jnp.int32 if whole else BF16)
            for two, three, whole in ((1, 0, 0), (0, 0, 0), (0, 0, 0), (0, 0, 1), (0, 1, 0))
        ]

    x_first, x_last, y_first, y_last = pl.pallas_call(
        edge_kernel,
        name="edges",
        out_shape=(jax.ShapeDtypeStruct((7, ny, nz), BF16),) * 2
        + (jax.ShapeDtypeStruct((7, nx, nz), BF16),) * 2,
        in_specs=[HBM] * 5,
        out_specs=(vmem,) * 4,
        scratch_shapes=pieces((ny, nz))
        + pieces((nx, TOP, nz))
        + [
            vm((7, 16 * TOP, nz), F32),
            vm((16 * TOP, nz), jnp.int32),
            pltpu.SemaphoreType.DMA((2, 5)),
            pltpu.SemaphoreType.DMA((2, 5, cuts)),
        ],
        compiler_params=PARAMS,
        cost_estimate=pl.CostEstimate(
            flops=20 * nx * nz, bytes_accessed=200 * nx * nz, transcendentals=0
        ),
    )(c, p, d, s, u)
    x_fwd, x_bwd = rings("stream")
    y_fwd, y_bwd = rings("tile")
    low_x = lax.ppermute(x_last, "stream", x_fwd)
    high_x = lax.ppermute(x_first, "stream", x_bwd)
    low_y = lax.ppermute(y_last, "tile", y_fwd)
    high_y = lax.ppermute(y_first, "tile", y_bwd)
    return low_x, high_x, low_y, high_y


def roll_lanes(value, shift):
    return pltpu.roll(value, shift % value.shape[-1], axis=value.ndim - 1)


def face(low, high):
    f = low[3] * high[3]
    h = f * (high[2] - low[2])
    a = f + h
    b = f - h
    return a * high[0] - b * low[0], b * high[1] - a * low[1]


def onehot(rows, cols, test):
    r = lax.broadcasted_iota(jnp.int32, (rows, cols), 0)
    c = lax.broadcasted_iota(jnp.int32, (rows, cols), 1)
    return jnp.where(test(r, c), 1.0, 0.0)


def ion_kernel(capacity, inner, *refs):
    refs = list(refs)
    plan, me, c_hbm, p_hbm, d_hbm, s_hbm = refs[:6]
    refs = refs[6:]
    edges_hbm = []
    if not inner:
        edges_hbm, refs = refs[:4], refs[5:]
    cn_hbm, out_hbm, c_v, p_v, d_v, s_v = refs[:6]
    refs = refs[6:]
    if not inner:
        xl_v, xh_v, yl_v, yh_v, yl_f, yh_f = refs[:6]
        refs = refs[6:]
    fld, cn_v, chs, blk, zero, perm, lanes, shift, shift2, dpot = refs[:10]
    tally, in_sem, halo_sem, cn_sem, blk_sem, zero_sem = refs[10:]
    nx, _, nz = p_hbm.shape
    chunks = nx // BLK
    bz = nz // BLK
    slots = out_hbm.shape[0]
    tiles = slots // capacity
    count = chunks * bz
    m0, m1 = TOP, BLK - TOP
    first = m0 - 1 if inner else 0
    depth = m1 + 1 - first if inner else BLK

    def loads(i):
        part = pl.ds(i * BLK + first, depth)
        return (
            pltpu.make_async_copy(c_hbm.at[:, part], c_v.at[:, part], in_sem.at[0, i]),
            pltpu.make_async_copy(p_hbm.at[part], p_v.at[part], in_sem.at[1, i]),
            pltpu.make_async_copy(d_hbm.at[part], d_v.at[part], in_sem.at[2, i]),
            pltpu.make_async_copy(s_hbm.at[part], s_v.at[part], in_sem.at[3, i]),
        )

    halos = []
    if not inner:
        for n, (src, dst) in enumerate(zip(edges_hbm, (xl_v, xh_v, yl_v, yh_v))):
            halos.append(pltpu.make_async_copy(src.at[pl.ds(0, 4)], dst, halo_sem.at[n]))
    for copy in halos:
        copy.start()
    for i in range(chunks):
        for copy in loads(i):
            copy.start()

    zero[...] = jnp.zeros_like(zero)
    width = BLK * TOP
    if not inner:
        perm[1] = onehot(
            width, width, lambda r, c: (r // BLK == c % TOP) & (r % BLK == c // TOP)
        ).astype(BF16)
    half = BLK // 2
    perm[0] = onehot(
        width,
        width,
        lambda r, c: (r // half == (c // (half * TOP)) * TOP + c % TOP)
        & (r % half == (c // TOP) % half),
    ).astype(BF16)
    wide = bz * nz
    lanes[...] = onehot(
        wide,
        wide,
        lambda r, c: (r // nz == (c % nz) // BLK) & (r % nz == (c // nz) * BLK + c % BLK),
    ).astype(BF16)
    near = onehot(
        nz, 2 * nz, lambda r, c: ((c < nz) & (r == c - 1)) | ((c >= nz) & (r == c - nz + 1))
    )
    own = onehot(nz, 2 * nz, lambda r, c: r == c % nz)
    shift[...] = near.astype(BF16)
    shift2[0:nz, :] = near.astype(BF16)
    shift2[nz : 2 * nz, :] = near.astype(BF16)
    dpot[...] = (near - own).astype(BF16)

    @pl.loop(0, tiles)
    def _(o):
        tally[count + o] = 0

    def place(o):
        return o if inner else lax.rem(o + tiles - me[0], tiles)

    @pl.loop(0, count)
    def _(b):
        o = place(plan[b])
        rank = tally[count + o]
        tally[b] = o * capacity + rank
        tally[count + o] = rank + 1

    def blank(slot):
        return pltpu.make_async_copy(zero, out_hbm.at[slot], zero_sem.at[slot])

    @pl.loop(0, tiles)
    def _(o):
        @pl.loop(tally[count + o], capacity)
        def _(k):
            blank(o * capacity + k).start()

    body = pl.ds(TOP, BLK)

    def scaled(f, v):
        v = v.astype(F32)
        if f == 2:
            return v * 0.5
        return v * lax.rsqrt(jnp.maximum(v, 0.25)) if f == 3 else v

    if not inner:
        for copy in halos:
            copy.wait()
        for plane, ref in ((0, xl_v), (nx + 1, xh_v)):
            for f in range(4):
                fld[f, plane, body, :] = scaled(f, ref[f])
        for ref, dst in ((yl_v, yl_f), (yh_v, yh_f)):
            for f in range(4):
                dst[f] = scaled(f, ref[f])

    def convert(x, number):
        at = pl.ds(x, number)
        to = pl.ds(x + 1, number)
        fld[0, to, body, :] = c_v[0, at].astype(F32)
        fld[1, to, body, :] = c_v[1, at].astype(F32)
        fld[2, to, body, :] = p_v[at].astype(F32) * 0.5
        d = d_v[at].astype(F32)
        fld[3, to, body, :] = jnp.where(s_v[at] > 0, d * lax.rsqrt(d), 0.0)

    def prepare(i):
        for copy in loads(i):
            copy.wait()
        if inner:
            convert(i * BLK + first, 1)
            convert(i * BLK + m1, 1)

            @pl.loop(m0 // 4, m1 // 4)
            def _(q):
                convert(i * BLK + q * 4, 4)

            return

        @pl.loop(0, BLK // 4)
        def _(q):
            x = i * BLK + q * 4
            convert(x, 4)
            for j in range(4):
                for f in range(4):
                    fld[f, x + 1 + j, pl.ds(TOP - 1, 1), :] = yl_f[f, pl.ds(x + j, 1), :]
                    fld[f, x + 1 + j, pl.ds(TOP + BLK, 1), :] = yh_f[f, pl.ds(x + j, 1), :]

    batch = TOP

    def planes(x, number, row, tall):
        return [fld[f, pl.ds(x + 1, number), pl.ds(TOP + row, tall), :] for f in range(4)]

    def update(x, row, tall):
        mid = planes(x, batch, row, tall)
        c0, c1, pot, s = mid
        m = batch * tall

        def flat(v):
            return v.reshape(m, nz)

        high = s.astype(BF16)
        low = (s - high.astype(F32)).astype(BF16)
        both = jnp.concatenate([flat(c0), flat(c1)], axis=0).astype(BF16)
        zc = jnp.dot(both, shift[...], preferred_element_type=F32)
        zs = jnp.dot(
            jnp.concatenate([flat(high), flat(low)], axis=1),
            shift2[...],
            preferred_element_type=F32,
        )
        zp = jnp.dot(flat(pot).astype(BF16), dpot[...], preferred_element_type=F32)
        lows = planes(x - 1, batch + 1, row, tall)
        highs = planes(x, batch + 1, row, tall)
        fx = face(lows, highs)
        total = [fx[sp][1:] - fx[sp][:batch] for sp in range(2)]
        sides = []
        for off in (-1, 1):
            n0, n1, npot, ns = planes(x, batch, row + off, tall)
            sides.append((n0, n1, npot - pot, ns))
        for part in (slice(0, nz), slice(nz, 2 * nz)):
            parts = (zc[:m, part], zc[m:, part], zp[:, part], zs[:, part])
            sides.append(tuple(v.reshape(batch, tall, nz) for v in parts))
        sum_a = sum_b = None
        for n0, n1, dp, ns in sides:
            f = s * ns
            h = f * dp
            a = f + h
            b = f - h
            total[0] = total[0] + n0 * a
            total[1] = total[1] + n1 * b
            sum_a = a if sum_a is None else sum_a + a
            sum_b = b if sum_b is None else sum_b + b
        total[0] = total[0] - c0 * sum_b
        total[1] = total[1] - c1 * sum_a
        new = []
        for sp in range(2):
            value = mid[sp] + (ion_step * species_diff[sp]) * total[sp]
            new.append(value.astype(BF16))
            cn_v[sp, pl.ds(x, batch), pl.ds(row, tall), :] = new[sp]
        return (new[0].astype(F32) - new[1].astype(F32)).astype(BF16)

    def keep(group, offset, charge):
        m = charge.shape[0] * charge.shape[1]
        at = pl.multiple_of(offset, m) if not isinstance(offset, int) else offset
        chs[group, pl.ds(at, m), :] = charge.reshape(m, nz)

    def saves(i):
        x = i * BLK
        spots = [(m0, m1 - m0, m0, m1 - m0)]
        if not inner:
            spots = [(0, BLK, 0, TOP), (0, BLK, m1, TOP), (0, m0, m0, m1 - m0)]
            spots.append((m1, TOP, m0, m1 - m0))
        copies = []
        for n, (px, number, row, tall) in enumerate(spots):
            at = (slice(None), pl.ds(x + px, number), pl.ds(row, tall))
            copies.append(pltpu.make_async_copy(cn_v.at[at], cn_hbm.at[at], cn_sem.at[n, i]))
        return copies

    def put(b):
        return pltpu.make_async_copy(blk.at[b], out_hbm.at[tally[b]], blk_sem.at[b])

    def joined(t, size):
        groups = t.shape[0] // (size * bz)
        return [
            jnp.concatenate(
                [t[(j * bz + m) * size : (j * bz + m + 1) * size] for m in range(bz)], axis=1
            )
            for j in range(groups)
        ]

    prepare(0)

    @pl.loop(0, chunks)
    def _(i):
        @pl.when(i + 1 < chunks)
        def _():
            prepare(i + 1)

        x = i * BLK
        middle = half * TOP
        if inner:

            @pl.loop(0, (m1 - m0) // batch)
            def _(q):
                charge = update(x + m0 + q * batch, m0, m1 - m0)
                for t in range(2):
                    keep(0, t * middle + q * batch * TOP, charge[:, t * TOP : (t + 1) * TOP])

        else:

            @pl.loop(0, BLK // batch)
            def _(q):
                for t, row in enumerate((0, m1)):
                    keep(1 + t, q * batch * TOP, update(x + q * batch, row, TOP))

            for q, px in enumerate((0, m1)):
                charge = update(x + px, m0, m1 - m0)
                for t in range(2):
                    keep(0, t * middle + q * batch * TOP, charge[:, t * TOP : (t + 1) * TOP])

        for copy in saves(i):
            copy.start()
        rowsets = []
        if not inner:
            for t in range(2):
                v = jnp.dot(perm[1], chs[1 + t], preferred_element_type=F32).astype(BF16)
                rowsets += joined(v, BLK)
        v = jnp.dot(perm[0], chs[0], preferred_element_type=F32).astype(BF16)
        rowsets += joined(v, half)
        res = jnp.dot(
            jnp.concatenate(rowsets, axis=0), lanes[...], preferred_element_type=F32
        ).astype(BF16)
        groups = TOP // bz
        for k in range(bz):
            row = 0
            if not inner:
                for j in range(2 * groups):
                    blk[i * bz + k, 0:BLK, j * nz : (j + 1) * nz] = res[
                        row : row + BLK, k * nz : (k + 1) * nz
                    ]
                    row += BLK
            base = 0 if inner else BLK
            for j in range(2 * groups):
                blk[i * bz + k, base : base + half, j * nz : (j + 1) * nz] = res[
                    row : row + half, k * nz : (k + 1) * nz
                ]
                row += half
            put(i * bz + k).start()

    @pl.loop(0, chunks)
    def _(i):
        for copy in saves(i):
            copy.wait()

    @pl.loop(0, count)
    def _(b):
        put(b).wait()

    @pl.loop(0, tiles)
    def _(o):
        @pl.loop(tally[count + o], capacity)
        def _(k):
            blank(o * capacity + k).wait()


def ion_call(plan, me, c, p, d, s, halo, before, capacity, tiles):
    _, nx, ny, nz = c.shape
    count = plan.shape[0]
    chunks = nx // BLK
    bz = nz // BLK
    inner = before is None
    args = [plan, me, c, p, d, s] + ([] if inner else list(halo) + [before])
    deep = BLK // 2 if inner else BLK + BLK // 2
    wide = BLK * BLK // 2
    vm = pltpu.VMEM
    dma = pltpu.SemaphoreType.DMA
    ends = [
        vm((4, ny, nz), BF16),
        vm((4, ny, nz), BF16),
        vm((4, nx, nz), BF16),
        vm((4, nx, nz), BF16),
        vm((4, nx, nz), F32),
        vm((4, nx, nz), F32),
    ]
    share = 0.25 if inner else 0.75
    return pl.pallas_call(
        functools.partial(ion_kernel, capacity, inner),
        name="ion_inner" if inner else "ion_outer",
        out_shape=(
            jax.ShapeDtypeStruct(c.shape, BF16),
            jax.ShapeDtypeStruct((tiles * capacity, deep, wide), BF16),
        ),
        in_specs=[pl.BlockSpec(memory_space=pltpu.SMEM)] * 2 + [HBM] * (len(args) - 2),
        out_specs=(HBM, HBM),
        scratch_shapes=[
            vm(c.shape, BF16),
            vm(p.shape, BF16),
            vm(p.shape, BF16),
            vm(p.shape, jnp.int32),
        ]
        + ([] if inner else ends)
        + [
            vm((4, nx + 2, ROWS, nz), F32),
            vm(c.shape, BF16),
            vm((1 if inner else 3, BLK * TOP, nz), BF16),
            vm((count, deep, wide), BF16),
            vm((deep, wide), BF16),
            vm((2, BLK * TOP, BLK * TOP), BF16),
            vm((bz * nz, bz * nz), BF16),
            vm((nz, 2 * nz), BF16),
            vm((2 * nz, 2 * nz), BF16),
            vm((nz, 2 * nz), BF16),
            pltpu.SMEM((count + tiles,), jnp.int32),
            dma((4, chunks)),
            dma((4,)),
            dma((4, chunks)),
            dma((count,)),
            dma((tiles * capacity,)),
        ],
        input_output_aliases={} if inner else {len(args) - 1: 0},
        compiler_params=PARAMS,
        cost_estimate=pl.CostEstimate(
            flops=int(100 * p.size * share),
            bytes_accessed=int(60 * p.size * share),
            transcendentals=int(p.size * share),
        ),
    )(*args)


def gather_kernel(boxes, capacity, shifts, aliased, *refs):
    me, parts, refs = refs[0], refs[1 : 1 + len(shifts)], refs[1 + len(shifts) + aliased :]
    out_hbm, sem = refs
    tiles = out_hbm.shape[0] // capacity

    def moves(n):
        base = lax.rem(me[0] + (tiles - shifts[n]), tiles) * capacity
        at = pl.ds(base, parts[n].shape[0])
        copies = []
        for m, ((r0, l0), (x0, y0), rows, width) in enumerate(boxes):
            copies.append(
                pltpu.make_async_copy(
                    parts[n].at[:, pl.ds(r0, rows), pl.ds(l0, width)],
                    out_hbm.at[at, pl.ds(x0, rows), pl.ds(y0, width)],
                    sem.at[n, m],
                )
            )
        return copies

    for n in range(len(shifts)):
        for copy in moves(n):
            copy.start()
    for n in range(len(shifts)):
        for copy in moves(n):
            copy.wait()


def gather_call(me, parts, shifts, inner, before, slots, capacity):
    q, h = BLK * BLK // 4, BLK // 2
    t = TOP
    if inner:
        boxes = (((0, 0), (t, q), h, 2 * q),)
    else:
        boxes = (
            ((0, 0), (0, 0), BLK, q),
            ((0, q), (0, 3 * q), BLK, q),
            ((BLK, 0), (0, q), t, 2 * q),
            ((BLK + t, 0), (BLK - t, q), t, 2 * q),
        )
    vmem = pl.BlockSpec(memory_space=pltpu.VMEM)
    args = [me] + list(parts) + ([] if before is None else [before])
    return pl.pallas_call(
        functools.partial(gather_kernel, boxes, capacity, shifts, before is not None),
        name="gather_inner" if inner else "gather_outer",
        out_shape=jax.ShapeDtypeStruct((slots, BLK, BLK * BLK), BF16),
        in_specs=[pl.BlockSpec(memory_space=pltpu.SMEM)]
        + [vmem] * len(parts)
        + [HBM] * (before is not None),
        out_specs=HBM,
        scratch_shapes=[pltpu.SemaphoreType.DMA((len(parts), len(boxes)))],
        input_output_aliases={} if before is None else {len(args) - 1: 0},
        compiler_params=pltpu.CompilerParams(vmem_limit_bytes=8 * 2**20),
        cost_estimate=pl.CostEstimate(
            flops=0, bytes_accessed=4 * sum(v.size for v in parts), transcendentals=0
        ),
    )(*args)


def flow_kernel(
    u_hbm,
    p_hbm,
    s_hbm,
    cn_hbm,
    xl_hbm,
    xh_hbm,
    yl_hbm,
    yh_hbm,
    un_hbm,
    u_v,
    p_v,
    s_v,
    cn_v,
    uxl_v,
    uxh_v,
    uyl_v,
    uyh_v,
    pxl_v,
    pxh_v,
    pyl_v,
    pyh_v,
    yl_f,
    yh_f,
    fld,
    un_v,
    in_sem,
    halo_sem,
    un_sem,
):
    nx, nz = p_hbm.shape[0], p_hbm.shape[2]
    chunks = nx // BLK

    def loads(i):
        part = pl.ds(i * BLK, BLK)
        return (
            pltpu.make_async_copy(u_hbm.at[:, part], u_v.at[:, part], in_sem.at[0, i]),
            pltpu.make_async_copy(p_hbm.at[part], p_v.at[part], in_sem.at[1, i]),
            pltpu.make_async_copy(s_hbm.at[part], s_v.at[part], in_sem.at[2, i]),
            pltpu.make_async_copy(cn_hbm.at[:, part], cn_v.at[:, part], in_sem.at[3, i]),
        )

    pairs = (
        (xl_hbm, uxl_v),
        (xh_hbm, uxh_v),
        (yl_hbm, uyl_v),
        (yh_hbm, uyh_v),
        (xl_hbm, pxl_v),
        (xh_hbm, pxh_v),
        (yl_hbm, pyl_v),
        (yh_hbm, pyh_v),
    )
    halos = [
        pltpu.make_async_copy(src.at[2] if n > 3 else src.at[pl.ds(4, 3)], dst, halo_sem.at[n])
        for n, (src, dst) in enumerate(pairs)
    ]
    for copy in halos:
        copy.start()
    for i in range(chunks):
        for copy in loads(i):
            copy.start()
    for copy in halos:
        copy.wait()
    body = pl.ds(TOP, BLK)
    for plane, ref, pref in ((0, uxl_v, pxl_v), (nx + 1, uxh_v, pxh_v)):
        for f in range(3):
            fld[f, plane, body, :] = ref[f].astype(F32)
        fld[3, plane, body, :] = pref[...].astype(F32)
    for ref, pref, dst in ((uyl_v, pyl_v, yl_f), (uyh_v, pyh_v, yh_f)):
        for f in range(3):
            dst[f] = ref[f].astype(F32)
        dst[3] = pref[...].astype(F32)

    def prepare(i):
        for copy in loads(i):
            copy.wait()

        @pl.loop(0, BLK)
        def _(q):
            x = i * BLK + q
            fluid = s_v[x] > 0
            for f in range(3):
                fld[f, x + 1, body, :] = jnp.where(fluid, u_v[f, x].astype(F32), 0.0)
            fld[3, x + 1, body, :] = p_v[x].astype(F32)
            for f in range(4):
                fld[f, x + 1, pl.ds(TOP - 1, 1), :] = yl_f[f, pl.ds(x, 1), :]
                fld[f, x + 1, pl.ds(TOP + BLK, 1), :] = yh_f[f, pl.ds(x, 1), :]

    half = 16
    lane = lax.broadcasted_iota(jnp.int32, (half, nz), 1)
    first_lane = lane == 0
    last_lane = lane == nz - 1
    k_mid = flow_step * viscosity
    k_adv = flow_step * 0.5

    def below(v):
        return jnp.where(first_lane, 0.0, roll_lanes(v, 1))

    def above(v):
        return jnp.where(last_lane, 0.0, roll_lanes(v, -1))

    def update(i):
        @pl.loop(0, BLK)
        def _(q):
            x = i * BLK + q
            for y0 in range(0, BLK, half):
                at = pl.ds(TOP + y0, half)
                mid = [fld[f, x + 1, at, :] for f in range(3)]
                field = fld[3, x + 1, at, :]
                fluid = s_v[x, pl.ds(y0, half), :] > 0
                cn0 = cn_v[0, x, pl.ds(y0, half), :].astype(F32)
                cn1 = cn_v[1, x, pl.ds(y0, half), :].astype(F32)
                push = (cn0 - cn1) * k_adv
                plus = [k_mid - k_adv * u for u in mid]
                minus = [k_mid + k_adv * u for u in mid]
                for a in range(3):
                    total = mid[a] * (1.0 - 6.0 * k_mid)
                    total = total + fld[a, x + 2, at, :] * plus[0] + fld[a, x, at, :] * minus[0]
                    total = total + fld[a, x + 1, pl.ds(TOP + 1 + y0, half), :] * plus[1]
                    total = total + fld[a, x + 1, pl.ds(TOP - 1 + y0, half), :] * minus[1]
                    total = total + above(mid[a]) * plus[2] + below(mid[a]) * minus[2]
                    if a == 0:
                        rise = fld[3, x + 2, at, :] - fld[3, x, at, :]
                    elif a == 1:
                        rise = (
                            fld[3, x + 1, pl.ds(TOP + 1 + y0, half), :]
                            - fld[3, x + 1, pl.ds(TOP - 1 + y0, half), :]
                        )
                    else:
                        rise = above(field) - below(field)
                    total = jnp.where(fluid, total - push * rise, 0.0)
                    un_v[a, x, pl.ds(y0, half), :] = total.astype(BF16)

    def saves(i):
        part = pl.ds(i * BLK, BLK)
        return pltpu.make_async_copy(un_v.at[:, part], un_hbm.at[:, part], un_sem.at[i])

    prepare(0)

    @pl.loop(0, chunks)
    def _(i):
        @pl.when(i + 1 < chunks)
        def _():
            prepare(i + 1)

        update(i)
        saves(i).start()

    @pl.loop(0, chunks)
    def _(i):
        saves(i).wait()


def flow_call(u, p, s, cn, halo):
    _, nx, ny, nz = u.shape
    chunks = nx // BLK
    vm = pltpu.VMEM
    dma = pltpu.SemaphoreType.DMA
    return pl.pallas_call(
        flow_kernel,
        name="flow",
        out_shape=jax.ShapeDtypeStruct(u.shape, BF16),
        in_specs=[HBM] * 8,
        out_specs=HBM,
        scratch_shapes=[
            vm(u.shape, BF16),
            vm(p.shape, BF16),
            vm(s.shape, jnp.int32),
            vm(cn.shape, BF16),
            vm((3, ny, nz), BF16),
            vm((3, ny, nz), BF16),
            vm((3, nx, nz), BF16),
            vm((3, nx, nz), BF16),
            vm((ny, nz), BF16),
            vm((ny, nz), BF16),
            vm((nx, nz), BF16),
            vm((nx, nz), BF16),
            vm((4, nx, nz), F32),
            vm((4, nx, nz), F32),
            vm((4, nx + 2, ROWS, nz), F32),
            vm(u.shape, BF16),
            dma((4, chunks)),
            dma((8,)),
            dma((chunks,)),
        ],
        compiler_params=PARAMS,
        cost_estimate=pl.CostEstimate(
            flops=80 * p.size, bytes_accessed=20 * p.size, transcendentals=0
        ),
    )(u, p, s, cn, *halo)


def per_device(concentration, potential, diffusivity, spacer, velocity, balance_plan):
    tiles = lax.axis_size("tile")
    count = balance_plan.shape[0]
    capacity = max(2, (2 * count + tiles - 1) // tiles)
    slots = tiles * capacity

    me = lax.axis_index("tile").astype(jnp.int32)[None]

    def exchange(part):
        part = part.reshape((tiles, capacity) + part.shape[1:])
        part = lax.all_to_all(part, "tile", split_axis=0, concat_axis=0, tiled=True)
        return part.reshape((slots,) + part.shape[2:])

    def pass_on(part, shift):
        piece = part[shift * capacity : (shift + 1) * capacity]
        if shift == 0:
            return piece
        return lax.ppermute(piece, "tile", [(i, (i + shift) % tiles) for i in range(tiles)])

    halo = edges(concentration, potential, diffusivity, spacer, velocity)
    given = (balance_plan[:, 0], me, concentration, potential, diffusivity, spacer)
    conc, first = ion_call(*given, None, None, capacity, tiles)
    first = exchange(first)
    conc_next, second = ion_call(*given, halo, conc, capacity, tiles)
    order = sorted(range(1, tiles), key=lambda d: -min(d, tiles - d)) + [0]
    pieces = [pass_on(second, d) for d in order]
    flow_next = flow_call(velocity, potential, spacer, conc_next, halo)
    owned = gather_call(jnp.zeros_like(me), [first], (0,), True, None, slots, capacity)
    owned = gather_call(me, pieces, tuple(order), False, owned, slots, capacity)
    return conc_next, flow_next, owned


def solution(mesh):
    placed = (
        P(None, "stream", "tile", None),
        P("stream", "tile", None),
        P("stream", "tile", None),
        P("stream", "tile", None),
        P(None, "stream", "tile", None),
        P(("stream", "tile"), None),
    )
    return jax.shard_map(
        per_device,
        mesh=mesh,
        in_specs=placed,
        out_specs=(
            P(None, "stream", "tile", None),
            P(None, "stream", "tile", None),
            P(("stream", "tile"), None, None),
        ),
        check_vma=False,
    )
```

```python
import functools

import jax
import jax.numpy as jnp
from jax import lax
from jax.experimental import pallas as pl
from jax.experimental.pallas import tpu as pltpu
from jax.sharding import PartitionSpec as P


BLK = 32
TOP = 8
ROWS = 48

ion_step = 0.04
flow_step = 0.1
viscosity = 0.5
species_diff = (1.0, 1.5)

F32 = jnp.float32
BF16 = jnp.bfloat16

HBM = pl.BlockSpec(memory_space=pltpu.HBM)
VMEM = pl.BlockSpec(memory_space=pltpu.VMEM)
SMEM = pl.BlockSpec(memory_space=pltpu.SMEM)
PARAMS = pltpu.CompilerParams(vmem_limit_bytes=60 * 2**20)


def rings(axis):
    count = lax.axis_size(axis)
    forward = [(i, (i + 1) % count) for i in range(count)]
    backward = [(target, source) for source, target in forward]
    return forward, backward


def edge_kernel(*refs):
    c_hbm, p_hbm, d_hbm, s_hbm, u_hbm, first, last = refs[:7]
    c_y, p_y, d_y, s_y, u_y, tmp, tmp_s, y_sem = refs[7:]
    nx, ny, nz = p_hbm.shape
    cuts = y_sem.shape[2]
    step = nx // cuts

    def rows(n, i):
        part = pl.ds(i * step, step)
        row = pl.ds(0 if n == 0 else ny - TOP, TOP)
        copies = []
        pairs = zip((c_hbm, p_hbm, d_hbm, s_hbm, u_hbm), (c_y, p_y, d_y, s_y, u_y))
        for j, (src, dst) in enumerate(pairs):
            if len(src.shape) == 4:
                pair = src.at[:, part, row], dst.at[n, :, part]
            else:
                pair = src.at[part, row], dst.at[n, part]
            copies.append(pltpu.make_async_copy(*pair, y_sem.at[n, j, i]))
        return copies

    for i in range(cuts):
        for n in range(2):
            for copy in rows(n, i):
                copy.start()
    size = 16
    for i in range(cuts):
        for n, out in enumerate((first, last)):
            for copy in rows(n, i):
                copy.wait()
            row = 0 if n == 0 else TOP - 1

            @pl.loop(0, step // size)
            def _(q, i=i, n=n, out=out, row=row):
                at = pl.ds(pl.multiple_of(i * step + q * size, size), size)
                picked = pl.ds(row, size, stride=TOP)
                tmp_s[...] = s_y[n, at].reshape(size * TOP, nz)
                solid = tmp_s[picked, :] > 0
                loaded = [c_y[n, 0, at], c_y[n, 1, at], p_y[n, at], d_y[n, at]]
                loaded += [u_y[n, f, at] for f in range(3)]
                for f, v in enumerate(loaded):
                    tmp[f] = v.astype(F32).reshape(size * TOP, nz)
                for f in range(7):
                    v = tmp[f, picked, :]
                    if f > 2:
                        v = jnp.where(solid, v, 0.0)
                    out[f, at, :] = v.astype(BF16)


def field_scratch(shape):
    leads = ((2, 2), (2,), (2,), (2,), (2, 3))
    kinds = (BF16, BF16, BF16, jnp.int32, BF16)
    return [pltpu.VMEM(lead + shape, kind) for lead, kind in zip(leads, kinds)]


def edge_call(c, p, d, s, u):
    nx, _, nz = p.shape
    cuts = 4
    return pl.pallas_call(
        edge_kernel,
        name="edges",
        out_shape=(jax.ShapeDtypeStruct((7, nx, nz), BF16),) * 2,
        in_specs=[HBM] * 5,
        out_specs=(VMEM,) * 2,
        scratch_shapes=field_scratch((nx, TOP, nz))
        + [
            pltpu.VMEM((7, 16 * TOP, nz), F32),
            pltpu.VMEM((16 * TOP, nz), jnp.int32),
            pltpu.SemaphoreType.DMA((2, 5, cuts)),
        ],
        compiler_params=PARAMS,
        cost_estimate=pl.CostEstimate(
            flops=20 * nx * nz, bytes_accessed=200 * nx * nz, transcendentals=0
        ),
    )(c, p, d, s, u)


def swap_ends(first, last, axis):
    forward, backward = rings(axis)
    return lax.ppermute(last, axis, forward), lax.ppermute(first, axis, backward)


def face(low, high):
    f = low[3] * high[3]
    h = f * (high[2] - low[2])
    a = f + h
    b = f - h
    return a * high[0] - b * low[0], b * high[1] - a * low[1]


def onehot(rows, cols, test):
    r = lax.broadcasted_iota(jnp.int32, (rows, cols), 0)
    c = lax.broadcasted_iota(jnp.int32, (rows, cols), 1)
    return jnp.where(test(r, c), 1.0, 0.0)


def ion_kernel(capacity, mode, spread, *refs):
    inner, mid, outer = mode == "inner", mode == "mid", mode == "outer"
    refs = list(refs)

    def take(number):
        taken = refs[:number]
        del refs[:number]
        return taken

    plan, me, c_hbm, p_hbm, d_hbm, s_hbm = take(6)
    nx, _, nz = p_hbm.shape
    chunks = nx // BLK
    bz = nz // BLK
    count = chunks * bz
    u_hbm = take(1)[0] if inner else None
    edges_hbm = [] if inner else take(4 if outer else 2)
    take(0 if inner else 1)
    cn_hbm = take(1)[0]
    outs = take(spread)
    ends = take(2 if inner else 0)
    c_v, p_v, d_v, s_v = take(4)
    raw = take(5 if inner else 0)
    edges_v = take(len(edges_hbm))
    edges_f = take(2 if outer else 0)
    fld, cn_v, chs, blk, zero, perm, lanes, shift, shift2, dpot = take(10)
    tally, in_sem, halo_sem, cn_sem, blk_sem, zero_sem = refs
    tiles = zero_sem.shape[0] // capacity
    m0, m1 = TOP, BLK - TOP
    first = m0 - 1 if inner else 0
    depth = m1 + 1 - first if inner else BLK

    def loads(i):
        part = pl.ds(i * BLK + first, depth)
        return (
            pltpu.make_async_copy(c_hbm.at[:, part], c_v.at[:, part], in_sem.at[0, i]),
            pltpu.make_async_copy(p_hbm.at[part], p_v.at[part], in_sem.at[1, i]),
            pltpu.make_async_copy(d_hbm.at[part], d_v.at[part], in_sem.at[2, i]),
            pltpu.make_async_copy(s_hbm.at[part], s_v.at[part], in_sem.at[3, i]),
        )

    halos = [
        pltpu.make_async_copy(src.at[pl.ds(0, 4)], dst, halo_sem.at[n])
        for n, (src, dst) in enumerate(zip(edges_hbm, edges_v))
    ]
    if inner:
        for j, (src, dst) in enumerate(zip((c_hbm, p_hbm, d_hbm, s_hbm, u_hbm), raw)):
            for n in range(2):
                at = n * (nx - 1)
                part = src.at[:, at] if len(src.shape) == 4 else src.at[at]
                halos.append(pltpu.make_async_copy(part, dst.at[n], halo_sem.at[2 * j + n]))
    else:
        for copy in halos:
            copy.start()
    for i in range(chunks):
        for copy in loads(i):
            copy.start()
    if inner:
        for copy in halos:
            copy.start()

    zero[...] = jnp.zeros_like(zero)
    width = BLK * TOP
    if outer:
        perm[0] = onehot(
            width, width, lambda r, c: (r // BLK == c % TOP) & (r % BLK == c // TOP)
        ).astype(BF16)
    half = BLK // 2
    if not outer:
        perm[0] = onehot(
            width,
            width,
            lambda r, c: (r // half == (c // (half * TOP)) * TOP + c % TOP)
            & (r % half == (c // TOP) % half),
        ).astype(BF16)
    wide = bz * nz
    lanes[...] = onehot(
        wide,
        wide,
        lambda r, c: (r // nz == (c % nz) // BLK) & (r % nz == (c // nz) * BLK + c % BLK),
    ).astype(BF16)
    near = onehot(
        nz, 2 * nz, lambda r, c: ((c < nz) & (r == c - 1)) | ((c >= nz) & (r == c - nz + 1))
    )
    own = onehot(nz, 2 * nz, lambda r, c: r == c % nz)
    shift[...] = near.astype(BF16)
    shift2[0:nz, :] = near.astype(BF16)
    shift2[nz : 2 * nz, :] = near.astype(BF16)
    dpot[...] = (near - own).astype(BF16)

    @pl.loop(0, tiles)
    def _(o):
        tally[count + o] = 0

    def place(o):
        return o if spread == 1 else lax.rem(o + tiles - me[0], tiles)

    @pl.loop(0, count)
    def _(b):
        o = place(plan[b])
        rank = tally[count + o]
        tally[b] = rank if spread > 1 else o * capacity + rank
        tally[count + o] = rank + 1

    def blank(o, k, ref=None):
        if spread == 1:
            return pltpu.make_async_copy(
                zero, outs[0].at[o * capacity + k], zero_sem.at[o * capacity + k]
            )
        return pltpu.make_async_copy(zero, ref.at[k], zero_sem.at[o * capacity + k])

    def blanks(act):
        if spread == 1:

            @pl.loop(0, tiles)
            def _(o):
                @pl.loop(tally[count + o], capacity)
                def _(k):
                    act(blank(o, k))

            return
        for o in range(tiles):

            @pl.loop(tally[count + o], capacity)
            def _(k, o=o):
                act(blank(o, k, outs[o]))

    blanks(lambda copy: copy.start())

    body = pl.ds(TOP, BLK)

    def scaled(f, v):
        v = v.astype(F32)
        if f == 2:
            return v * 0.5
        return v * lax.rsqrt(jnp.maximum(v, 0.25)) if f == 3 else v

    if not inner:
        for copy in halos:
            copy.wait()
        for plane, ref in zip((0, nx + 1), edges_v):
            for f in range(4):
                fld[f, plane, body, :] = scaled(f, ref[f])
        for ref, dst in zip(edges_v[2:], edges_f):
            for f in range(4):
                dst[f] = scaled(f, ref[f])

    def convert(x, number):
        at = pl.ds(x, number)
        to = pl.ds(x + 1, number)
        fld[0, to, body, :] = c_v[0, at].astype(F32)
        fld[1, to, body, :] = c_v[1, at].astype(F32)
        fld[2, to, body, :] = p_v[at].astype(F32) * 0.5
        d = d_v[at].astype(F32)
        fld[3, to, body, :] = jnp.where(s_v[at] > 0, d * lax.rsqrt(d), 0.0)

    def prepare(i):
        for copy in loads(i):
            copy.wait()
        if not outer:
            convert(i * BLK + m0 - 1, 1)
            convert(i * BLK + m0, 1) if mid else None
            convert(i * BLK + m1 - 1, 1) if mid else None
            convert(i * BLK + m1, 1)

            @pl.loop(0, 4)
            def _(q):
                shifted = q * 4 + (m0 if inner else jnp.where(q >= 2, m1 - m0, 0))
                convert(i * BLK + shifted, 4)

            return

        @pl.loop(0, BLK // 4)
        def _(q):
            x = i * BLK + q * 4
            convert(x, 4)
            for j in range(4):
                for f in range(4):
                    for n, row in enumerate((TOP - 1, TOP + BLK)):
                        fld[f, x + 1 + j, pl.ds(row, 1), :] = edges_f[n][f, pl.ds(x + j, 1), :]

    batch = TOP

    def planes(x, number, row, tall):
        return [fld[f, pl.ds(x + 1, number), pl.ds(TOP + row, tall), :] for f in range(4)]

    def update(x, row, tall):
        mid = planes(x, batch, row, tall)
        c0, c1, pot, s = mid
        m = batch * tall

        def flat(v):
            return v.reshape(m, nz)

        high = s.astype(BF16)
        low = (s - high.astype(F32)).astype(BF16)
        both = jnp.concatenate([flat(c0), flat(c1)], axis=0).astype(BF16)
        zc = jnp.dot(both, shift[...], preferred_element_type=F32)
        zs = jnp.dot(
            jnp.concatenate([flat(high), flat(low)], axis=1),
            shift2[...],
            preferred_element_type=F32,
        )
        zp = jnp.dot(flat(pot).astype(BF16), dpot[...], preferred_element_type=F32)
        lows = planes(x - 1, batch + 1, row, tall)
        highs = planes(x, batch + 1, row, tall)
        fx = face(lows, highs)
        total = [fx[sp][1:] - fx[sp][:batch] for sp in range(2)]
        sides = []
        for off in (-1, 1):
            n0, n1, npot, ns = planes(x, batch, row + off, tall)
            sides.append((n0, n1, npot - pot, ns))
        for part in (slice(0, nz), slice(nz, 2 * nz)):
            parts = (zc[:m, part], zc[m:, part], zp[:, part], zs[:, part])
            sides.append(tuple(v.reshape(batch, tall, nz) for v in parts))
        sum_a = sum_b = None
        for n0, n1, dp, ns in sides:
            f = s * ns
            h = f * dp
            a = f + h
            b = f - h
            total[0] = total[0] + n0 * a
            total[1] = total[1] + n1 * b
            sum_a = a if sum_a is None else sum_a + a
            sum_b = b if sum_b is None else sum_b + b
        total[0] = total[0] - c0 * sum_b
        total[1] = total[1] - c1 * sum_a
        new = []
        for sp in range(2):
            value = mid[sp] + (ion_step * species_diff[sp]) * total[sp]
            new.append(value.astype(BF16))
            cn_v[sp, pl.ds(x, batch), pl.ds(row, tall), :] = new[sp]
        return (new[0].astype(F32) - new[1].astype(F32)).astype(BF16)

    def keep(group, offset, charge):
        m = charge.shape[0] * charge.shape[1]
        at = pl.multiple_of(offset, m) if not isinstance(offset, int) else offset
        chs[group, pl.ds(at, m), :] = charge.reshape(m, nz)

    def saves(i):
        x = i * BLK
        spots = [(m0, m1 - m0, m0, m1 - m0)]
        if mid:
            spots = [(0, m0, m0, m1 - m0), (m1, TOP, m0, m1 - m0)]
        if outer:
            spots = [(0, BLK, 0, TOP), (0, BLK, m1, TOP)]
        copies = []
        for n, (px, number, row, tall) in enumerate(spots):
            at = (slice(None), pl.ds(x + px, number), pl.ds(row, tall))
            copies.append(pltpu.make_async_copy(cn_v.at[at], cn_hbm.at[at], cn_sem.at[n, i]))
        return copies

    def put(b, n=0):
        return pltpu.make_async_copy(blk.at[b], outs[n].at[tally[b]], blk_sem.at[b])

    def send(b):
        if spread == 1:
            put(b).start()
            return
        shift = place(plan[b])
        for n in range(tiles):

            @pl.when(shift == n)
            def _(n=n):
                put(b, n).start()

    def joined(t, size):
        groups = t.shape[0] // (size * bz)
        return [
            jnp.concatenate(
                [t[(j * bz + m) * size : (j * bz + m + 1) * size] for m in range(bz)], axis=1
            )
            for j in range(groups)
        ]

    prepare(0)

    @pl.loop(0, chunks)
    def _(i):
        @pl.when(i + 1 < chunks)
        def _():
            prepare(i + 1)

        x = i * BLK
        middle = half * TOP
        if inner:

            @pl.loop(0, (m1 - m0) // batch)
            def _(q):
                charge = update(x + m0 + q * batch, m0, m1 - m0)
                for t in range(2):
                    keep(0, t * middle + q * batch * TOP, charge[:, t * TOP : (t + 1) * TOP])

        if mid:

            @pl.loop(0, 2)
            def _(q):
                charge = update(x + q * m1, m0, m1 - m0)
                for t in range(2):
                    keep(0, t * middle + q * batch * TOP, charge[:, t * TOP : (t + 1) * TOP])

        if outer:

            @pl.loop(0, BLK // batch)
            def _(q):
                for t, row in enumerate((0, m1)):
                    keep(t, q * batch * TOP, update(x + q * batch, row, TOP))

        for copy in saves(i):
            copy.start()
        size = BLK if outer else half
        rowsets = []
        for t in range(2 if outer else 1):
            v = jnp.dot(perm[0], chs[t], preferred_element_type=F32).astype(BF16)
            rowsets += joined(v, size)
        res = jnp.dot(
            jnp.concatenate(rowsets, axis=0), lanes[...], preferred_element_type=F32
        ).astype(BF16)
        for k in range(bz):
            for j in range(len(rowsets)):
                blk[i * bz + k, :, j * nz : (j + 1) * nz] = res[
                    j * size : (j + 1) * size, k * nz : (k + 1) * nz
                ]
            send(i * bz + k)

    if inner:
        for copy in halos:
            copy.wait()
        c_x, p_x, d_x, s_x, u_x = raw
        for n, out in enumerate(ends):
            solid = s_x[n] > 0
            out[0] = c_x[n, 0]
            out[1] = c_x[n, 1]
            out[2] = p_x[n]
            out[3] = jnp.where(solid, d_x[n].astype(F32), 0.0).astype(BF16)
            for f in range(3):
                out[4 + f] = jnp.where(solid, u_x[n, f].astype(F32), 0.0).astype(BF16)

    @pl.loop(0, chunks)
    def _(i):
        for copy in saves(i):
            copy.wait()

    @pl.loop(0, count)
    def _(b):
        put(b).wait()

    blanks(lambda copy: copy.wait())


def ion_call(mode, plan, me, c, p, d, s, u, halo, before, capacity, tiles):
    _, nx, ny, nz = c.shape
    count = plan.shape[0]
    chunks = nx // BLK
    bz = nz // BLK
    inner, outer = mode == "inner", mode == "outer"
    args = [plan, me, c, p, d, s] + ([u] if inner else list(halo) + [before])
    deep = BLK if outer else BLK // 2
    wide = BLK * BLK // 2
    spread = tiles if outer else 1
    vm = pltpu.VMEM
    dma = pltpu.SemaphoreType.DMA
    extra = field_scratch((ny, nz)) if inner else [vm((4, ny, nz), BF16)] * 2
    if outer:
        extra += [vm((4, nx, nz), BF16)] * 2 + [vm((4, nx, nz), F32)] * 2
    share = 0.5 if outer else 0.25
    part = jax.ShapeDtypeStruct((tiles * capacity // spread, deep, wide), BF16)
    end = jax.ShapeDtypeStruct((7, ny, nz), BF16)
    return pl.pallas_call(
        functools.partial(ion_kernel, capacity, mode, spread),
        out_shape=[jax.ShapeDtypeStruct(c.shape, BF16)] + [part] * spread + [end] * (2 * inner),
        in_specs=[SMEM] * 2 + [HBM] * (len(args) - 2),
        out_specs=[HBM] * (1 + spread) + [VMEM] * (2 * inner),
        scratch_shapes=[
            vm(c.shape, BF16),
            vm(p.shape, BF16),
            vm(p.shape, BF16),
            vm(p.shape, jnp.int32),
        ]
        + extra
        + [
            vm((4, nx + 2, ROWS, nz), F32),
            vm(c.shape, BF16),
            vm((2 if outer else 1, BLK * TOP, nz), BF16),
            vm((count, deep, wide), BF16),
            vm((deep, wide), BF16),
            vm((1, BLK * TOP, BLK * TOP), BF16),
            vm((bz * nz, bz * nz), BF16),
            vm((nz, 2 * nz), BF16),
            vm((2 * nz, 2 * nz), BF16),
            vm((nz, 2 * nz), BF16),
            pltpu.SMEM((count + tiles,), jnp.int32),
            dma((4, chunks)),
            dma((10,)),
            dma((2, chunks)),
            dma((count,)),
            dma((tiles * capacity,)),
        ],
        input_output_aliases={} if inner else {len(args) - 1: 0},
        compiler_params=PARAMS,
        cost_estimate=pl.CostEstimate(
            flops=int(100 * p.size * share),
            bytes_accessed=int(60 * p.size * share),
            transcendentals=int(p.size * share),
        ),
    )(*args)


def gather_kernel(boxes, capacity, shifts, aliased, *refs):
    me, parts, refs = refs[0], refs[1 : 1 + len(shifts)], refs[1 + len(shifts) + aliased :]
    out_hbm, sem = refs
    tiles = out_hbm.shape[0] // capacity

    def moves(n):
        base = lax.rem(me[0] + (tiles - shifts[n]), tiles) * capacity
        at = pl.ds(base, parts[n].shape[0])
        copies = []
        for m, ((r0, l0), (x0, y0), rows, width) in enumerate(boxes):
            copies.append(
                pltpu.make_async_copy(
                    parts[n].at[:, pl.ds(r0, rows), pl.ds(l0, width)],
                    out_hbm.at[at, pl.ds(x0, rows), pl.ds(y0, width)],
                    sem.at[n, m],
                )
            )
        return copies

    for n in range(len(shifts)):
        for copy in moves(n):
            copy.start()
    for n in range(len(shifts)):
        for copy in moves(n):
            copy.wait()


def gather_call(mode, me, parts, shifts, before, slots, capacity):
    q, h = BLK * BLK // 4, BLK // 2
    t = TOP
    boxes = {
        "inner": (((0, 0), (t, q), h, 2 * q),),
        "mid": (((0, 0), (0, q), t, 2 * q), ((t, 0), (BLK - t, q), t, 2 * q)),
        "outer": (((0, 0), (0, 0), BLK, q), ((0, q), (0, 3 * q), BLK, q)),
    }[mode]
    args = [me] + list(parts) + ([] if before is None else [before])
    return pl.pallas_call(
        functools.partial(gather_kernel, boxes, capacity, shifts, before is not None),
        out_shape=jax.ShapeDtypeStruct((slots, BLK, BLK * BLK), BF16),
        in_specs=[SMEM]
        + [VMEM] * len(parts)
        + [HBM] * (before is not None),
        out_specs=HBM,
        scratch_shapes=[pltpu.SemaphoreType.DMA((len(parts), len(boxes)))],
        input_output_aliases={} if before is None else {len(args) - 1: 0},
        compiler_params=pltpu.CompilerParams(vmem_limit_bytes=8 * 2**20),
        cost_estimate=pl.CostEstimate(
            flops=0, bytes_accessed=4 * sum(v.size for v in parts), transcendentals=0
        ),
    )(*args)


def flow_kernel(
    u_hbm,
    p_hbm,
    s_hbm,
    cn_hbm,
    xl_hbm,
    xh_hbm,
    yl_hbm,
    yh_hbm,
    un_hbm,
    u_v,
    p_v,
    s_v,
    cn_v,
    uxl_v,
    uxh_v,
    uyl_v,
    uyh_v,
    pxl_v,
    pxh_v,
    pyl_v,
    pyh_v,
    yl_f,
    yh_f,
    fld,
    un_v,
    mix,
    in_sem,
    halo_sem,
    un_sem,
):
    nx, nz = p_hbm.shape[0], p_hbm.shape[2]
    chunks = nx // BLK

    def loads(i):
        part = pl.ds(i * BLK, BLK)
        return (
            pltpu.make_async_copy(u_hbm.at[:, part], u_v.at[:, part], in_sem.at[0, i]),
            pltpu.make_async_copy(p_hbm.at[part], p_v.at[part], in_sem.at[1, i]),
            pltpu.make_async_copy(s_hbm.at[part], s_v.at[part], in_sem.at[2, i]),
            pltpu.make_async_copy(cn_hbm.at[:, part], cn_v.at[:, part], in_sem.at[3, i]),
        )

    pairs = (
        (xl_hbm, uxl_v),
        (xh_hbm, uxh_v),
        (yl_hbm, uyl_v),
        (yh_hbm, uyh_v),
        (xl_hbm, pxl_v),
        (xh_hbm, pxh_v),
        (yl_hbm, pyl_v),
        (yh_hbm, pyh_v),
    )
    halos = [
        pltpu.make_async_copy(src.at[2] if n > 3 else src.at[pl.ds(4, 3)], dst, halo_sem.at[n])
        for n, (src, dst) in enumerate(pairs)
    ]
    for copy in halos:
        copy.start()
    for i in range(chunks):
        for copy in loads(i):
            copy.start()
    for copy in halos:
        copy.wait()
    body = pl.ds(TOP, BLK)
    for plane, ref, pref in ((0, uxl_v, pxl_v), (nx + 1, uxh_v, pxh_v)):
        for f in range(3):
            fld[f, plane, body, :] = ref[f].astype(F32)
        fld[3, plane, body, :] = pref[...].astype(F32)
    for ref, pref, dst in ((uyl_v, pyl_v, yl_f), (uyh_v, pyh_v, yh_f)):
        for f in range(3):
            dst[f] = ref[f].astype(F32)
        dst[3] = pref[...].astype(F32)

    def prepare(i):
        for copy in loads(i):
            copy.wait()

        @pl.loop(0, BLK)
        def _(q):
            x = i * BLK + q
            fluid = s_v[x] > 0
            for f in range(3):
                fld[f, x + 1, body, :] = jnp.where(fluid, u_v[f, x].astype(F32), 0.0)
            fld[3, x + 1, body, :] = p_v[x].astype(F32)
            for f in range(4):
                fld[f, x + 1, pl.ds(TOP - 1, 1), :] = yl_f[f, pl.ds(x, 1), :]
                fld[f, x + 1, pl.ds(TOP + BLK, 1), :] = yh_f[f, pl.ds(x, 1), :]

    up = onehot(nz, nz, lambda r, c: r == c + 1)
    down = onehot(nz, nz, lambda r, c: r == c - 1)
    mix[:, 0:nz] = ((up + down) * viscosity).astype(BF16)
    mix[:, nz : 2 * nz] = ((up - down) * 0.5).astype(BF16)
    batch, tall = 4, 16

    def update(i):
        @pl.loop(0, BLK // batch)
        def _(q):
            x = i * BLK + q * batch
            here = pl.ds(x + 1, batch)
            for y0 in range(0, BLK, tall):
                at = pl.ds(TOP + y0, tall)
                next_y, last_y = pl.ds(TOP + 1 + y0, tall), pl.ds(TOP - 1 + y0, tall)
                own = pl.ds(y0, tall)
                mid = [fld[f, here, at, :] for f in range(4)]
                m = batch * tall
                stack = jnp.concatenate([v.reshape(m, nz) for v in mid], axis=0).astype(BF16)
                z = jnp.dot(stack, mix[...], preferred_element_type=F32)
                z = [z[f * m : (f + 1) * m] for f in range(4)]
                fluid = s_v[pl.ds(x, batch), own, :] > 0
                push = cn_v[0, pl.ds(x, batch), own, :].astype(F32)
                push = (push - cn_v[1, pl.ds(x, batch), own, :].astype(F32)) * 0.5
                plus = [viscosity - 0.5 * u for u in mid[:2]]
                minus = [viscosity + 0.5 * u for u in mid[:2]]
                for a in range(3):
                    total = fld[a, pl.ds(x + 2, batch), at, :] * plus[0]
                    total = total + fld[a, pl.ds(x, batch), at, :] * minus[0]
                    total = total + fld[a, here, next_y, :] * plus[1]
                    total = total + fld[a, here, last_y, :] * minus[1]
                    total = total + z[a][:, :nz].reshape(batch, tall, nz)
                    total = total - mid[2] * z[a][:, nz:].reshape(batch, tall, nz)
                    if a == 0:
                        rise = fld[3, pl.ds(x + 2, batch), at, :] - fld[3, pl.ds(x, batch), at, :]
                    elif a == 1:
                        rise = fld[3, here, next_y, :] - fld[3, here, last_y, :]
                    else:
                        rise = z[3][:, nz:].reshape(batch, tall, nz) * 2.0
                    total = total - push * rise
                    value = mid[a] * (1.0 - 6.0 * viscosity * flow_step) + flow_step * total
                    value = jnp.where(fluid, value, 0.0)
                    un_v[a, pl.ds(x, batch), own, :] = value.astype(BF16)

    def saves(i):
        part = pl.ds(i * BLK, BLK)
        return pltpu.make_async_copy(un_v.at[:, part], un_hbm.at[:, part], un_sem.at[i])

    prepare(0)

    @pl.loop(0, chunks)
    def _(i):
        @pl.when(i + 1 < chunks)
        def _():
            prepare(i + 1)

        update(i)
        saves(i).start()

    @pl.loop(0, chunks)
    def _(i):
        saves(i).wait()


def flow_call(u, p, s, cn, halo):
    _, nx, ny, nz = u.shape
    chunks = nx // BLK
    vm = pltpu.VMEM
    dma = pltpu.SemaphoreType.DMA
    return pl.pallas_call(
        flow_kernel,
        name="flow",
        out_shape=jax.ShapeDtypeStruct(u.shape, BF16),
        in_specs=[HBM] * 8,
        out_specs=HBM,
        scratch_shapes=[
            vm(u.shape, BF16),
            vm(p.shape, BF16),
            vm(s.shape, jnp.int32),
            vm(cn.shape, BF16),
            vm((3, ny, nz), BF16),
            vm((3, ny, nz), BF16),
            vm((3, nx, nz), BF16),
            vm((3, nx, nz), BF16),
            vm((ny, nz), BF16),
            vm((ny, nz), BF16),
            vm((nx, nz), BF16),
            vm((nx, nz), BF16),
            vm((4, nx, nz), F32),
            vm((4, nx, nz), F32),
            vm((4, nx + 2, ROWS, nz), F32),
            vm(u.shape, BF16),
            vm((nz, 2 * nz), BF16),
            dma((4, chunks)),
            dma((8,)),
            dma((chunks,)),
        ],
        compiler_params=PARAMS,
        cost_estimate=pl.CostEstimate(
            flops=80 * p.size, bytes_accessed=20 * p.size, transcendentals=0
        ),
    )(u, p, s, cn, *halo)


def per_device(concentration, potential, diffusivity, spacer, velocity, balance_plan):
    tiles = lax.axis_size("tile")
    count = balance_plan.shape[0]
    capacity = max(2, (2 * count + tiles - 1) // tiles)
    slots = tiles * capacity

    me = lax.axis_index("tile").astype(jnp.int32)[None]

    def exchange(part):
        part = part.reshape((tiles, capacity) + part.shape[1:])
        part = lax.all_to_all(part, "tile", split_axis=0, concat_axis=0, tiled=True)
        return part.reshape((slots,) + part.shape[2:])

    def pass_on(piece, shift):
        if shift == 0:
            return piece
        return lax.ppermute(piece, "tile", [(i, (i + shift) % tiles) for i in range(tiles)])

    given = (balance_plan[:, 0], me, concentration, potential, diffusivity, spacer, velocity)
    conc, first, x_first, x_last = ion_call("inner", *given, None, None, capacity, tiles)
    first = exchange(first)
    x_halo = swap_ends(x_first, x_last, "stream")
    y_first, y_last = edge_call(*given[2:])
    y_halo = swap_ends(y_first, y_last, "tile")
    conc, second = ion_call("mid", *given, x_halo, conc, capacity, tiles)
    second = exchange(second)
    halo = x_halo + y_halo
    conc_next, *third = ion_call("outer", *given, halo, conc, capacity, tiles)
    order = sorted(range(1, tiles), key=lambda d: -min(d, tiles - d)) + [0]
    third = [pass_on(third[d], d) for d in order]
    flow_next = flow_call(velocity, potential, spacer, conc_next, halo)
    none = jnp.zeros_like(me)
    owned = gather_call("inner", none, [first], (0,), None, slots, capacity)
    owned = gather_call("mid", none, [second], (0,), owned, slots, capacity)
    owned = gather_call("outer", me, third, tuple(order), owned, slots, capacity)
    return conc_next, flow_next, owned


def solution(mesh):
    placed = (
        P(None, "stream", "tile", None),
        P("stream", "tile", None),
        P("stream", "tile", None),
        P("stream", "tile", None),
        P(None, "stream", "tile", None),
        P(("stream", "tile"), None),
    )
    return jax.shard_map(
        per_device,
        mesh=mesh,
        in_specs=placed,
        out_specs=(
            P(None, "stream", "tile", None),
            P(None, "stream", "tile", None),
            P(("stream", "tile"), None, None),
        ),
        check_vma=False,
    )
```

```python
import functools

import jax
import jax.numpy as jnp
from jax import lax
from jax.experimental import pallas as pl
from jax.experimental.pallas import tpu as pltpu
from jax.sharding import PartitionSpec as P


BLK = 32
TOP = 8
ROWS = 48
AHEAD = 2

ion_step = 0.04
flow_step = 0.1
viscosity = 0.5
species_diff = (1.0, 1.5)

F32 = jnp.float32
BF16 = jnp.bfloat16

HBM = pl.BlockSpec(memory_space=pltpu.HBM)
VMEM = pl.BlockSpec(memory_space=pltpu.VMEM)
SMEM = pl.BlockSpec(memory_space=pltpu.SMEM)
PARAMS = pltpu.CompilerParams(vmem_limit_bytes=60 * 2**20)


def rings(axis):
    count = lax.axis_size(axis)
    forward = [(i, (i + 1) % count) for i in range(count)]
    backward = [(target, source) for source, target in forward]
    return forward, backward


def field_scratch(shape):
    leads = ((2, 2), (2,), (2,), (2,), (2, 3))
    kinds = (BF16, BF16, BF16, jnp.int32, BF16)
    return [pltpu.VMEM(lead + shape, kind) for lead, kind in zip(leads, kinds)]


def swap_ends(first, last, axis):
    forward, backward = rings(axis)
    return lax.ppermute(last, axis, forward), lax.ppermute(first, axis, backward)


def face(low, high):
    f = low[3] * high[3]
    h = f * (high[2] - low[2])
    a = f + h
    b = f - h
    return a * high[0] - b * low[0], b * high[1] - a * low[1]


def onehot(rows, cols, test):
    r = lax.broadcasted_iota(jnp.int32, (rows, cols), 0)
    c = lax.broadcasted_iota(jnp.int32, (rows, cols), 1)
    return jnp.where(test(r, c), 1.0, 0.0)


def ion_kernel(capacity, mode, spread, *refs):
    inner, mid, outer = mode == "inner", mode == "mid", mode == "outer"
    refs = list(refs)

    def take(number):
        taken = refs[:number]
        del refs[:number]
        return taken

    plan, me, c_hbm, p_hbm, d_hbm, s_hbm = take(6)
    nx, ny, nz = p_hbm.shape
    chunks = nx // BLK
    bz = nz // BLK
    count = chunks * bz
    u_hbm = take(1)[0] if inner else None
    edges_hbm = [] if inner else take(4 if outer else 2)
    take(0 if inner else 1)
    cn_hbm = take(1)[0]
    outs = take(spread)
    ends = take(2 if inner else 0)
    rims = take(2 if inner else 0)
    c_v, p_v, d_v, s_v = take(4)
    raw = take(5 if inner else 0)
    rim_v = take(5 if inner else 0)
    tmp, tmp_s, rim_sem = take(3) if inner else (None, None, None)
    edges_v = take(len(edges_hbm))
    edges_f = take(2 if outer else 0)
    fld, cn_v, chs, blk, zero, perm, lanes, shift, shift2, dpot = take(10)
    tally, in_sem, halo_sem, cn_sem, blk_sem, zero_sem = refs
    tiles = zero_sem.shape[0] // capacity
    m0, m1 = TOP, BLK - TOP
    first = m0 - 1 if inner else 0
    depth = m1 + 1 - first if inner else BLK

    def loads(i):
        part = pl.ds(i * BLK + first, depth)
        return (
            pltpu.make_async_copy(c_hbm.at[:, part], c_v.at[:, part], in_sem.at[0, i]),
            pltpu.make_async_copy(p_hbm.at[part], p_v.at[part], in_sem.at[1, i]),
            pltpu.make_async_copy(d_hbm.at[part], d_v.at[part], in_sem.at[2, i]),
            pltpu.make_async_copy(s_hbm.at[part], s_v.at[part], in_sem.at[3, i]),
        )

    halos = [
        pltpu.make_async_copy(src.at[pl.ds(0, 4)], dst, halo_sem.at[n])
        for n, (src, dst) in enumerate(zip(edges_hbm, edges_v))
    ]
    if inner:
        for j, (src, dst) in enumerate(zip((c_hbm, p_hbm, d_hbm, s_hbm, u_hbm), raw)):
            for n in range(2):
                at = n * (nx - 1)
                part = src.at[:, at] if len(src.shape) == 4 else src.at[at]
                halos.append(pltpu.make_async_copy(part, dst.at[n], halo_sem.at[2 * j + n]))
    else:
        for copy in halos:
            copy.start()
    sources = (c_hbm, p_hbm, d_hbm, s_hbm, u_hbm)

    def rim_loads(i):
        part = pl.ds(i * BLK, BLK)
        copies = []
        for n in range(2):
            row = pl.ds(n * (ny - TOP), TOP)
            for j, (src, dst) in enumerate(zip(sources, rim_v)):
                if len(src.shape) == 4:
                    pair = src.at[:, part, row], dst.at[n, :, part]
                else:
                    pair = src.at[part, row], dst.at[n, part]
                copies.append(pltpu.make_async_copy(*pair, rim_sem.at[n, j, i]))
        return copies

    def rim(i, n, half_block):
        number = BLK // 2
        at = pl.ds(pl.multiple_of(i * BLK + half_block * number, number), number)
        picked = pl.ds(n * (TOP - 1), number, stride=TOP)
        spot = 2 * n + half_block
        c_y, p_y, d_y, s_y, u_y = rim_v
        tmp_s[spot] = s_y[n, at].reshape(number * TOP, nz)
        solid = tmp_s[spot, picked, :] > 0
        loaded = [c_y[n, 0, at], c_y[n, 1, at], p_y[n, at], d_y[n, at]]
        loaded += [u_y[n, f, at] for f in range(3)]
        for f, v in enumerate(loaded):
            tmp[spot, f] = v.astype(F32).reshape(number * TOP, nz)
        for f in range(7):
            v = tmp[spot, f, picked, :]
            if f > 2:
                v = jnp.where(solid, v, 0.0)
            rims[n][f, at, :] = v.astype(BF16)

    def fetch(i):
        for copy in loads(i):
            copy.start()
        if inner:
            for copy in rim_loads(i):
                copy.start()

    ahead = chunks if inner else min(AHEAD, chunks)
    for i in range(ahead):
        fetch(i)
    if inner:
        for copy in halos:
            copy.start()

    zero[...] = jnp.zeros_like(zero)
    width = BLK * TOP
    if outer:
        perm[0] = onehot(
            width, width, lambda r, c: (r // BLK == c % TOP) & (r % BLK == c // TOP)
        ).astype(BF16)
    half = BLK // 2
    if not outer:
        perm[0] = onehot(
            width,
            width,
            lambda r, c: (r // half == (c // (half * TOP)) * TOP + c % TOP)
            & (r % half == (c // TOP) % half),
        ).astype(BF16)
    wide = bz * nz
    lanes[...] = onehot(
        wide,
        wide,
        lambda r, c: (r // nz == (c % nz) // BLK) & (r % nz == (c // nz) * BLK + c % BLK),
    ).astype(BF16)
    near = onehot(
        nz, 2 * nz, lambda r, c: ((c < nz) & (r == c - 1)) | ((c >= nz) & (r == c - nz + 1))
    )
    own = onehot(nz, 2 * nz, lambda r, c: r == c % nz)
    shift[...] = near.astype(BF16)
    shift2[0:nz, :] = near.astype(BF16)
    shift2[nz : 2 * nz, :] = near.astype(BF16)
    dpot[...] = (near - own).astype(BF16)

    @pl.loop(0, tiles)
    def _(o):
        tally[count + o] = 0

    def place(o):
        return o if spread == 1 else lax.rem(o + tiles - me[0], tiles)

    @pl.loop(0, count)
    def _(b):
        o = place(plan[b])
        rank = tally[count + o]
        tally[b] = rank if spread > 1 else o * capacity + rank
        tally[count + o] = rank + 1

    def blank(o, k, ref=None):
        if spread == 1:
            return pltpu.make_async_copy(
                zero, outs[0].at[o * capacity + k], zero_sem.at[o * capacity + k]
            )
        return pltpu.make_async_copy(zero, ref.at[k], zero_sem.at[o * capacity + k])

    def blanks(act):
        if spread == 1:

            @pl.loop(0, tiles)
            def _(o):
                @pl.loop(tally[count + o], capacity)
                def _(k):
                    act(blank(o, k))

            return
        for o in range(tiles):

            @pl.loop(tally[count + o], capacity)
            def _(k, o=o):
                act(blank(o, k, outs[o]))

    blanks(lambda copy: copy.start())

    body = pl.ds(TOP, BLK)

    def scaled(f, v):
        v = v.astype(F32)
        if f == 2:
            return v * 0.5
        return v * lax.rsqrt(jnp.maximum(v, 0.25)) if f == 3 else v

    if not inner:
        for copy in halos:
            copy.wait()
        for plane, ref in zip((0, nx + 1), edges_v):
            for f in range(4):
                fld[f, plane, body, :] = scaled(f, ref[f])
        for ref, dst in zip(edges_v[2:], edges_f):
            for f in range(4):
                dst[f] = scaled(f, ref[f])

    def convert(x, number):
        at = pl.ds(x, number)
        to = pl.ds(x + 1, number)
        fld[0, to, body, :] = c_v[0, at].astype(F32)
        fld[1, to, body, :] = c_v[1, at].astype(F32)
        fld[2, to, body, :] = p_v[at].astype(F32) * 0.5
        d = d_v[at].astype(F32)
        fld[3, to, body, :] = jnp.where(s_v[at] > 0, d * lax.rsqrt(d), 0.0)

    def prepare(i):
        for copy in loads(i):
            copy.wait()
        if not outer:
            convert(i * BLK + m0 - 1, 1)
            convert(i * BLK + m0, 1) if mid else None
            convert(i * BLK + m1 - 1, 1) if mid else None
            convert(i * BLK + m1, 1)

            @pl.loop(0, 4)
            def _(q):
                shifted = q * 4 + (m0 if inner else jnp.where(q >= 2, m1 - m0, 0))
                convert(i * BLK + shifted, 4)

            return

        @pl.loop(0, BLK // 4)
        def _(q):
            x = i * BLK + q * 4
            convert(x, 4)
            for j in range(4):
                for f in range(4):
                    for n, row in enumerate((TOP - 1, TOP + BLK)):
                        fld[f, x + 1 + j, pl.ds(row, 1), :] = edges_f[n][f, pl.ds(x + j, 1), :]

    batch = TOP

    strips = ((0, TOP), (m1, TOP)) if outer else ((m0, m1 - m0),)
    tall = sum(number for _, number in strips)

    def planes(x, number, off=0):
        return [
            jnp.concatenate(
                [
                    fld[f, pl.ds(x + 1, number), pl.ds(TOP + row + off, rows), :]
                    for row, rows in strips
                ],
                axis=1,
            )
            for f in range(4)
        ]

    def update(x):
        m = batch * tall
        c0, c1, pot, s = [v.reshape(m, nz) for v in planes(x, batch)]
        high = s.astype(BF16)
        low = (s - high.astype(F32)).astype(BF16)
        zc = jnp.dot(
            jnp.concatenate([c0, c1], axis=0).astype(BF16),
            shift[...],
            preferred_element_type=F32,
        )
        zs = jnp.dot(
            jnp.concatenate([high, low], axis=1), shift2[...], preferred_element_type=F32
        )
        zp = jnp.dot(pot.astype(BF16), dpot[...], preferred_element_type=F32)

        def plane(j, off=0):
            return [v[0] for v in planes(x + j, 1, off)]

        mid = plane(0)
        below = face(plane(-1), mid)
        charges = []
        for j in range(batch):
            after = plane(j + 1)
            above = face(mid, after)
            total = [above[sp] - below[sp] for sp in range(2)]
            c0, c1, pot, s = mid
            sides = []
            for off in (-1, 1):
                n0, n1, npot, ns = plane(j, off)
                sides.append((n0, n1, npot - pot, ns))
            own = slice(j * tall, (j + 1) * tall)
            again = slice(m + j * tall, m + (j + 1) * tall)
            for part in (slice(0, nz), slice(nz, 2 * nz)):
                sides.append((zc[own, part], zc[again, part], zp[own, part], zs[own, part]))
            sum_a = sum_b = None
            for n0, n1, dp, ns in sides:
                f = s * ns
                h = f * dp
                a = f + h
                b = f - h
                total[0] = total[0] + n0 * a
                total[1] = total[1] + n1 * b
                sum_a = a if sum_a is None else sum_a + a
                sum_b = b if sum_b is None else sum_b + b
            total[0] = total[0] - c0 * sum_b
            total[1] = total[1] - c1 * sum_a
            new = []
            for sp in range(2):
                value = mid[sp] + (ion_step * species_diff[sp]) * total[sp]
                new.append(value.astype(BF16))
                at = 0
                for row, rows in strips:
                    cn_v[sp, x + j, pl.ds(row, rows), :] = new[sp][at : at + rows]
                    at += rows
            charges.append((new[0].astype(F32) - new[1].astype(F32)).astype(BF16)[None])
            mid, below = after, above
        return jnp.concatenate(charges, axis=0)

    def saves(i):
        x = i * BLK
        spots = [(m0, m1 - m0, m0, m1 - m0)]
        if mid:
            spots = [(0, m0, m0, m1 - m0), (m1, TOP, m0, m1 - m0)]
        if outer:
            spots = [(0, BLK, 0, TOP), (0, BLK, m1, TOP)]
        copies = []
        for n, (px, number, row, tall) in enumerate(spots):
            at = (slice(None), pl.ds(x + px, number), pl.ds(row, tall))
            copies.append(pltpu.make_async_copy(cn_v.at[at], cn_hbm.at[at], cn_sem.at[n, i]))
        return copies

    def put(b, n=0):
        return pltpu.make_async_copy(blk.at[b + bz], outs[n].at[tally[b]], blk_sem.at[b])

    def send(b):
        if spread == 1:
            put(b).start()
            return
        shift = place(plan[b])
        for n in range(tiles):

            @pl.when(shift == n)
            def _(n=n):
                put(b, n).start()

    def joined(t, size):
        groups = t.shape[0] // (size * bz)
        return [
            jnp.concatenate(
                [t[(j * bz + m) * size : (j * bz + m + 1) * size] for m in range(bz)], axis=1
            )
            for j in range(groups)
        ]

    offsets = {"inner": (m0, m0 + batch), "mid": (0, m1), "outer": range(0, BLK, batch)}[mode]
    size = BLK if outer else half

    def relayout(i):
        rowsets = []
        for t in range(2 if outer else 1):
            v = jnp.dot(perm[0], chs[t], preferred_element_type=F32).astype(BF16)
            rowsets += joined(v, size)
        res = jnp.dot(
            jnp.concatenate(rowsets, axis=0), lanes[...], preferred_element_type=F32
        ).astype(BF16)
        for k in range(bz):
            for j in range(len(rowsets)):
                blk[(i + 1) * bz + k, :, j * nz : (j + 1) * nz] = res[
                    j * size : (j + 1) * size, k * nz : (k + 1) * nz
                ]

    prepare(0)

    @pl.loop(0, chunks)
    def _(i):
        @pl.when(i + ahead < chunks)
        def _():
            fetch(i + ahead)

        @pl.when(i + 1 < chunks)
        def _():
            prepare(i + 1)

        if inner:
            for copy in rim_loads(i):
                copy.wait()
        relayout(i - 1)
        if inner:
            for n in range(2):
                for half_block in range(2):
                    rim(i, n, half_block)
        for q, offset in enumerate(offsets):
            charge = update(i * BLK + offset)
            m = batch * TOP
            for t in range(2):
                strip = charge[:, t * TOP : (t + 1) * TOP].reshape(m, nz)
                if outer:
                    chs[t, q * m : (q + 1) * m, :] = strip
                else:
                    at = t * half * TOP + q * m
                    chs[0, at : at + m, :] = strip
        for copy in saves(i):
            copy.start()

        @pl.when(i > 0)
        def _():
            for k in range(bz):
                send((i - 1) * bz + k)

    relayout(chunks - 1)
    for k in range(bz):
        send((chunks - 1) * bz + k)

    if inner:
        for copy in halos:
            copy.wait()
        c_x, p_x, d_x, s_x, u_x = raw
        for n, out in enumerate(ends):
            solid = s_x[n] > 0
            out[0] = c_x[n, 0]
            out[1] = c_x[n, 1]
            out[2] = p_x[n]
            out[3] = jnp.where(solid, d_x[n].astype(F32), 0.0).astype(BF16)
            for f in range(3):
                out[4 + f] = jnp.where(solid, u_x[n, f].astype(F32), 0.0).astype(BF16)

    @pl.loop(0, chunks)
    def _(i):
        for copy in saves(i):
            copy.wait()

    @pl.loop(0, count)
    def _(b):
        put(b).wait()

    blanks(lambda copy: copy.wait())


def ion_call(mode, plan, me, c, p, d, s, u, halo, before, capacity, tiles):
    _, nx, ny, nz = c.shape
    count = plan.shape[0]
    chunks = nx // BLK
    bz = nz // BLK
    inner, outer = mode == "inner", mode == "outer"
    args = [plan, me, c, p, d, s] + ([u] if inner else list(halo) + [before])
    deep = BLK if outer else BLK // 2
    wide = BLK * BLK // 2
    spread = tiles if outer else 1
    vm = pltpu.VMEM
    dma = pltpu.SemaphoreType.DMA
    extra = [vm((4, ny, nz), BF16)] * 2
    if inner:
        extra = field_scratch((ny, nz)) + field_scratch((nx, TOP, nz))
        extra += [vm((4, 7, BLK // 2 * TOP, nz), F32), vm((4, BLK // 2 * TOP, nz), jnp.int32)]
        extra.append(dma((2, 5, chunks)))
    if outer:
        extra += [vm((4, nx, nz), BF16)] * 2 + [vm((4, nx, nz), F32)] * 2
    share = 0.5 if outer else 0.25
    part = jax.ShapeDtypeStruct((tiles * capacity // spread, deep, wide), BF16)
    ends = [jax.ShapeDtypeStruct((7, number, nz), BF16) for number in (ny, ny, nx, nx)]
    ends = ends if inner else []
    return pl.pallas_call(
        functools.partial(ion_kernel, capacity, mode, spread),
        out_shape=[jax.ShapeDtypeStruct(c.shape, BF16)] + [part] * spread + ends,
        in_specs=[SMEM] * 2 + [HBM] * (len(args) - 2),
        out_specs=[HBM] * (1 + spread) + [VMEM] * len(ends),
        scratch_shapes=[
            vm(c.shape, BF16),
            vm(p.shape, BF16),
            vm(p.shape, BF16),
            vm(p.shape, jnp.int32),
        ]
        + extra
        + [
            vm((4, nx + 2, ROWS, nz), F32),
            vm(c.shape, BF16),
            vm((2 if outer else 1, BLK * TOP, nz), BF16),
            vm((count + bz, deep, wide), BF16),
            vm((deep, wide), BF16),
            vm((1, BLK * TOP, BLK * TOP), BF16),
            vm((bz * nz, bz * nz), BF16),
            vm((nz, 2 * nz), BF16),
            vm((2 * nz, 2 * nz), BF16),
            vm((nz, 2 * nz), BF16),
            pltpu.SMEM((count + tiles,), jnp.int32),
            dma((4, chunks)),
            dma((10,)),
            dma((2, chunks)),
            dma((count,)),
            dma((tiles * capacity,)),
        ],
        input_output_aliases={} if inner else {len(args) - 1: 0},
        compiler_params=pltpu.CompilerParams(vmem_limit_bytes=60 * 2**20),
        cost_estimate=pl.CostEstimate(
            flops=int(100 * p.size * share),
            bytes_accessed=int(60 * p.size * share),
            transcendentals=int(p.size * share),
        ),
    )(*args)


def gather_kernel(boxes, capacity, shifts, aliased, *refs):
    me, parts, refs = refs[0], refs[1 : 1 + len(shifts)], refs[1 + len(shifts) + aliased :]
    out_hbm, sem = refs
    tiles = out_hbm.shape[0] // capacity

    def moves(n):
        base = lax.rem(me[0] + (tiles - shifts[n]), tiles) * capacity
        at = pl.ds(base, parts[n].shape[0])
        copies = []
        for m, ((r0, l0), (x0, y0), rows, width) in enumerate(boxes):
            copies.append(
                pltpu.make_async_copy(
                    parts[n].at[:, pl.ds(r0, rows), pl.ds(l0, width)],
                    out_hbm.at[at, pl.ds(x0, rows), pl.ds(y0, width)],
                    sem.at[n, m],
                )
            )
        return copies

    for n in range(len(shifts)):
        for copy in moves(n):
            copy.start()
    for n in range(len(shifts)):
        for copy in moves(n):
            copy.wait()


def gather_call(mode, me, parts, shifts, before, slots, capacity):
    q, h = BLK * BLK // 4, BLK // 2
    t = TOP
    boxes = {
        "inner": (((0, 0), (t, q), h, 2 * q),),
        "mid": (((0, 0), (0, q), t, 2 * q), ((t, 0), (BLK - t, q), t, 2 * q)),
        "outer": (((0, 0), (0, 0), BLK, q), ((0, q), (0, 3 * q), BLK, q)),
    }[mode]
    args = [me] + list(parts) + ([] if before is None else [before])
    return pl.pallas_call(
        functools.partial(gather_kernel, boxes, capacity, shifts, before is not None),
        out_shape=jax.ShapeDtypeStruct((slots, BLK, BLK * BLK), BF16),
        in_specs=[SMEM]
        + [VMEM] * len(parts)
        + [HBM] * (before is not None),
        out_specs=HBM,
        scratch_shapes=[pltpu.SemaphoreType.DMA((len(parts), len(boxes)))],
        input_output_aliases={} if before is None else {len(args) - 1: 0},
        compiler_params=pltpu.CompilerParams(vmem_limit_bytes=8 * 2**20),
        cost_estimate=pl.CostEstimate(
            flops=0, bytes_accessed=4 * sum(v.size for v in parts), transcendentals=0
        ),
    )(*args)


def flow_kernel(
    u_hbm,
    p_hbm,
    s_hbm,
    cn_hbm,
    xl_hbm,
    xh_hbm,
    yl_hbm,
    yh_hbm,
    un_hbm,
    u_v,
    p_v,
    s_v,
    cn_v,
    uxl_v,
    uxh_v,
    uyl_v,
    uyh_v,
    pxl_v,
    pxh_v,
    pyl_v,
    pyh_v,
    yl_f,
    yh_f,
    fld,
    un_v,
    mix,
    in_sem,
    halo_sem,
    un_sem,
):
    nx, nz = p_hbm.shape[0], p_hbm.shape[2]
    chunks = nx // BLK

    def loads(i):
        part = pl.ds(i * BLK, BLK)
        return (
            pltpu.make_async_copy(u_hbm.at[:, part], u_v.at[:, part], in_sem.at[0, i]),
            pltpu.make_async_copy(p_hbm.at[part], p_v.at[part], in_sem.at[1, i]),
            pltpu.make_async_copy(s_hbm.at[part], s_v.at[part], in_sem.at[2, i]),
            pltpu.make_async_copy(cn_hbm.at[:, part], cn_v.at[:, part], in_sem.at[3, i]),
        )

    pairs = (
        (xl_hbm, uxl_v),
        (xh_hbm, uxh_v),
        (yl_hbm, uyl_v),
        (yh_hbm, uyh_v),
        (xl_hbm, pxl_v),
        (xh_hbm, pxh_v),
        (yl_hbm, pyl_v),
        (yh_hbm, pyh_v),
    )
    halos = [
        pltpu.make_async_copy(src.at[2] if n > 3 else src.at[pl.ds(4, 3)], dst, halo_sem.at[n])
        for n, (src, dst) in enumerate(pairs)
    ]
    for copy in halos:
        copy.start()
    for i in range(min(AHEAD, chunks)):
        for copy in loads(i):
            copy.start()
    for copy in halos:
        copy.wait()
    body = pl.ds(TOP, BLK)
    for plane, ref, pref in ((0, uxl_v, pxl_v), (nx + 1, uxh_v, pxh_v)):
        for f in range(3):
            fld[f, plane, body, :] = ref[f].astype(F32)
        fld[3, plane, body, :] = pref[...].astype(F32)
    for ref, pref, dst in ((uyl_v, pyl_v, yl_f), (uyh_v, pyh_v, yh_f)):
        for f in range(3):
            dst[f] = ref[f].astype(F32)
        dst[3] = pref[...].astype(F32)

    def prepare(i):
        for copy in loads(i):
            copy.wait()

        @pl.loop(0, BLK)
        def _(q):
            x = i * BLK + q
            fluid = s_v[x] > 0
            for f in range(3):
                fld[f, x + 1, body, :] = jnp.where(fluid, u_v[f, x].astype(F32), 0.0)
            fld[3, x + 1, body, :] = p_v[x].astype(F32)
            for f in range(4):
                fld[f, x + 1, pl.ds(TOP - 1, 1), :] = yl_f[f, pl.ds(x, 1), :]
                fld[f, x + 1, pl.ds(TOP + BLK, 1), :] = yh_f[f, pl.ds(x, 1), :]

    up = onehot(nz, nz, lambda r, c: r == c + 1)
    down = onehot(nz, nz, lambda r, c: r == c - 1)
    mix[:, 0:nz] = ((up + down) * viscosity).astype(BF16)
    mix[:, nz : 2 * nz] = ((up - down) * 0.5).astype(BF16)
    batch, tall = 4, 16

    def update(i):
        @pl.loop(0, BLK // batch)
        def _(q):
            x = i * BLK + q * batch
            here = pl.ds(x + 1, batch)
            for y0 in range(0, BLK, tall):
                at = pl.ds(TOP + y0, tall)
                next_y, last_y = pl.ds(TOP + 1 + y0, tall), pl.ds(TOP - 1 + y0, tall)
                own = pl.ds(y0, tall)
                mid = [fld[f, here, at, :] for f in range(4)]
                m = batch * tall
                stack = jnp.concatenate([v.reshape(m, nz) for v in mid], axis=0).astype(BF16)
                z = jnp.dot(stack, mix[...], preferred_element_type=F32)
                z = [z[f * m : (f + 1) * m] for f in range(4)]
                fluid = s_v[pl.ds(x, batch), own, :] > 0
                push = cn_v[0, pl.ds(x, batch), own, :].astype(F32)
                push = (push - cn_v[1, pl.ds(x, batch), own, :].astype(F32)) * 0.5
                plus = [viscosity - 0.5 * u for u in mid[:2]]
                minus = [viscosity + 0.5 * u for u in mid[:2]]
                for a in range(3):
                    total = fld[a, pl.ds(x + 2, batch), at, :] * plus[0]
                    total = total + fld[a, pl.ds(x, batch), at, :] * minus[0]
                    total = total + fld[a, here, next_y, :] * plus[1]
                    total = total + fld[a, here, last_y, :] * minus[1]
                    total = total + z[a][:, :nz].reshape(batch, tall, nz)
                    total = total - mid[2] * z[a][:, nz:].reshape(batch, tall, nz)
                    if a == 0:
                        rise = fld[3, pl.ds(x + 2, batch), at, :] - fld[3, pl.ds(x, batch), at, :]
                    elif a == 1:
                        rise = fld[3, here, next_y, :] - fld[3, here, last_y, :]
                    else:
                        rise = z[3][:, nz:].reshape(batch, tall, nz) * 2.0
                    total = total - push * rise
                    value = mid[a] * (1.0 - 6.0 * viscosity * flow_step) + flow_step * total
                    value = jnp.where(fluid, value, 0.0)
                    un_v[a, pl.ds(x, batch), own, :] = value.astype(BF16)

    def saves(i):
        part = pl.ds(i * BLK, BLK)
        return pltpu.make_async_copy(un_v.at[:, part], un_hbm.at[:, part], un_sem.at[i])

    prepare(0)

    @pl.loop(0, chunks)
    def _(i):
        @pl.when(i + AHEAD < chunks)
        def _():
            for copy in loads(i + AHEAD):
                copy.start()

        @pl.when(i + 1 < chunks)
        def _():
            prepare(i + 1)

        update(i)
        saves(i).start()

    @pl.loop(0, chunks)
    def _(i):
        saves(i).wait()


def flow_call(u, p, s, cn, halo):
    _, nx, ny, nz = u.shape
    chunks = nx // BLK
    vm = pltpu.VMEM
    dma = pltpu.SemaphoreType.DMA
    return pl.pallas_call(
        flow_kernel,
        name="flow",
        out_shape=jax.ShapeDtypeStruct(u.shape, BF16),
        in_specs=[HBM] * 8,
        out_specs=HBM,
        scratch_shapes=[
            vm(u.shape, BF16),
            vm(p.shape, BF16),
            vm(s.shape, jnp.int32),
            vm(cn.shape, BF16),
            vm((3, ny, nz), BF16),
            vm((3, ny, nz), BF16),
            vm((3, nx, nz), BF16),
            vm((3, nx, nz), BF16),
            vm((ny, nz), BF16),
            vm((ny, nz), BF16),
            vm((nx, nz), BF16),
            vm((nx, nz), BF16),
            vm((4, nx, nz), F32),
            vm((4, nx, nz), F32),
            vm((4, nx + 2, ROWS, nz), F32),
            vm(u.shape, BF16),
            vm((nz, 2 * nz), BF16),
            dma((4, chunks)),
            dma((8,)),
            dma((chunks,)),
        ],
        compiler_params=PARAMS,
        cost_estimate=pl.CostEstimate(
            flops=80 * p.size, bytes_accessed=20 * p.size, transcendentals=0
        ),
    )(u, p, s, cn, *halo)


def per_device(concentration, potential, diffusivity, spacer, velocity, balance_plan):
    tiles = lax.axis_size("tile")
    count = balance_plan.shape[0]
    capacity = max(2, (2 * count + tiles - 1) // tiles)
    slots = tiles * capacity

    me = lax.axis_index("tile").astype(jnp.int32)[None]

    def exchange(part):
        part = part.reshape((tiles, capacity) + part.shape[1:])
        part = lax.all_to_all(part, "tile", split_axis=0, concat_axis=0, tiled=True)
        return part.reshape((slots,) + part.shape[2:])

    def pass_on(piece, shift):
        if shift == 0:
            return piece
        return lax.ppermute(piece, "tile", [(i, (i + shift) % tiles) for i in range(tiles)])

    given = (balance_plan[:, 0], me, concentration, potential, diffusivity, spacer, velocity)
    conc, first, *ends = ion_call("inner", *given, None, None, capacity, tiles)
    first = exchange(first)
    x_halo = swap_ends(*ends[:2], "stream")
    y_halo = swap_ends(*ends[2:], "tile")
    conc, second = ion_call("mid", *given, x_halo, conc, capacity, tiles)
    second = exchange(second)
    halo = x_halo + y_halo
    conc_next, *third = ion_call("outer", *given, halo, conc, capacity, tiles)
    order = sorted(range(1, tiles), key=lambda d: -min(d, tiles - d)) + [0]
    third = [pass_on(third[d], d) for d in order]
    flow_next = flow_call(velocity, potential, spacer, conc_next, halo)
    none = jnp.zeros_like(me)
    owned = gather_call("inner", none, [first], (0,), None, slots, capacity)
    owned = gather_call("mid", none, [second], (0,), owned, slots, capacity)
    owned = gather_call("outer", me, third, tuple(order), owned, slots, capacity)
    return conc_next, flow_next, owned


def solution(mesh):
    placed = (
        P(None, "stream", "tile", None),
        P("stream", "tile", None),
        P("stream", "tile", None),
        P("stream", "tile", None),
        P(None, "stream", "tile", None),
        P(("stream", "tile"), None),
    )
    return jax.shard_map(
        per_device,
        mesh=mesh,
        in_specs=placed,
        out_specs=(
            P(None, "stream", "tile", None),
            P(None, "stream", "tile", None),
            P(("stream", "tile"), None, None),
        ),
        check_vma=False,
    )
```

```python
import functools

import jax
import jax.numpy as jnp
from jax import lax
from jax.experimental import pallas as pl
from jax.experimental.pallas import tpu as pltpu
from jax.sharding import PartitionSpec as P


BLK = 32
TOP = 8
ROWS = 48
AHEAD = 3

ion_step = 0.04
flow_step = 0.1
viscosity = 0.5
species_diff = (1.0, 1.5)

F32 = jnp.float32
BF16 = jnp.bfloat16

HBM = pl.BlockSpec(memory_space=pltpu.HBM)
VMEM = pl.BlockSpec(memory_space=pltpu.VMEM)
SMEM = pl.BlockSpec(memory_space=pltpu.SMEM)
PARAMS = pltpu.CompilerParams(vmem_limit_bytes=60 * 2**20)


def rings(axis):
    count = lax.axis_size(axis)
    forward = [(i, (i + 1) % count) for i in range(count)]
    backward = [(target, source) for source, target in forward]
    return forward, backward


def field_scratch(shape):
    leads = ((2, 2), (2,), (2,), (2,), (2, 3))
    kinds = (BF16, BF16, BF16, jnp.int32, BF16)
    return [pltpu.VMEM(lead + shape, kind) for lead, kind in zip(leads, kinds)]


def swap_ends(first, last, axis):
    forward, backward = rings(axis)
    return lax.ppermute(last, axis, forward), lax.ppermute(first, axis, backward)


def face(low, high):
    f = low[3] * high[3]
    h = f * (high[2] - low[2])
    a = f + h
    b = f - h
    return a * high[0] - b * low[0], b * high[1] - a * low[1]


def onehot(rows, cols, test):
    r = lax.broadcasted_iota(jnp.int32, (rows, cols), 0)
    c = lax.broadcasted_iota(jnp.int32, (rows, cols), 1)
    return jnp.where(test(r, c), 1.0, 0.0)


def ion_kernel(capacity, mode, spread, *refs):
    inner, mid, outer = mode == "inner", mode == "mid", mode == "outer"
    refs = list(refs)

    def take(number):
        taken = refs[:number]
        del refs[:number]
        return taken

    plan, me, c_hbm, p_hbm, d_hbm, s_hbm = take(6)
    nx, ny, nz = p_hbm.shape
    chunks = nx // BLK
    bz = nz // BLK
    count = chunks * bz
    u_hbm = take(1)[0] if inner else None
    edges_hbm = [] if inner else take(4 if outer else 2)
    take(0 if inner else 1)
    cn_hbm = take(1)[0]
    outs = take(spread)
    ends = take(2 if inner else 0)
    rims = take(4 if inner else 0)
    c_v, p_v, d_v, s_v = take(4)
    raw = take(5 if inner else 0)
    rim_v = take(5 if inner else 0)
    tmp, tmp_s, rim_sem = take(3) if inner else (None, None, None)
    edges_v = take(len(edges_hbm))
    edges_f = take(2 if outer else 0)
    fld, cn_v, chs, blk, zero, perm, lanes, shift, shift2, dpot = take(10)
    tally, in_sem, halo_sem, cn_sem, blk_sem, zero_sem = refs
    tiles = zero_sem.shape[0] // capacity
    m0, m1 = TOP, BLK - TOP
    first = m0 - 1 if inner else 0
    depth = m1 + 1 - first if inner else BLK

    def loads(i):
        part = pl.ds(i * BLK + first, depth)
        return (
            pltpu.make_async_copy(c_hbm.at[:, part], c_v.at[:, part], in_sem.at[0, i]),
            pltpu.make_async_copy(p_hbm.at[part], p_v.at[part], in_sem.at[1, i]),
            pltpu.make_async_copy(d_hbm.at[part], d_v.at[part], in_sem.at[2, i]),
            pltpu.make_async_copy(s_hbm.at[part], s_v.at[part], in_sem.at[3, i]),
        )

    halos = [
        pltpu.make_async_copy(src.at[pl.ds(0, 4)], dst, halo_sem.at[n])
        for n, (src, dst) in enumerate(zip(edges_hbm, edges_v))
    ]
    if inner:
        for j, (src, dst) in enumerate(zip((c_hbm, p_hbm, d_hbm, s_hbm, u_hbm), raw)):
            for n in range(2):
                at = n * (nx - 1)
                part = src.at[:, at] if len(src.shape) == 4 else src.at[at]
                halos.append(pltpu.make_async_copy(part, dst.at[n], halo_sem.at[2 * j + n]))
    else:
        for copy in halos:
            copy.start()
    sources = (c_hbm, p_hbm, d_hbm, s_hbm, u_hbm)

    def rim_loads(i):
        part = pl.ds(i * BLK, BLK)
        copies = []
        for n in range(2):
            row = pl.ds(n * (ny - TOP), TOP)
            for j, (src, dst) in enumerate(zip(sources, rim_v)):
                if len(src.shape) == 4:
                    pair = src.at[:, part, row], dst.at[n, :, part]
                else:
                    pair = src.at[part, row], dst.at[n, part]
                copies.append(pltpu.make_async_copy(*pair, rim_sem.at[n, j, i]))
        return copies

    def rim(i, n, half_block):
        number = BLK // 2
        at = pl.ds(pl.multiple_of(i * BLK + half_block * number, number), number)
        picked = pl.ds(n * (TOP - 1), number, stride=TOP)
        spot = 2 * n + half_block
        c_y, p_y, d_y, s_y, u_y = rim_v
        tmp_s[spot] = s_y[n, at].reshape(number * TOP, nz)
        solid = tmp_s[spot, picked, :] > 0
        loaded = [c_y[n, 0, at], c_y[n, 1, at], p_y[n, at], d_y[n, at]]
        loaded += [u_y[n, f, at] for f in range(3)]
        for f, v in enumerate(loaded):
            tmp[spot, f] = v.astype(F32).reshape(number * TOP, nz)
        for f in range(7):
            v = tmp[spot, f, picked, :]
            if f > 2:
                v = jnp.where(solid, v, 0.0)
            out, field = (rims[n], f) if f < 4 else (rims[2 + n], f - 4)
            out[field, at, :] = v.astype(BF16)

    def fetch(i):
        for copy in loads(i):
            copy.start()
        if inner:
            for copy in rim_loads(i):
                copy.start()

    ahead = chunks if inner else min(AHEAD, chunks)
    for i in range(ahead):
        fetch(i)
    if inner:
        for copy in halos:
            copy.start()

    zero[...] = jnp.zeros_like(zero)
    width = BLK * TOP
    if outer:
        perm[0] = onehot(
            width, width, lambda r, c: (r // BLK == c % TOP) & (r % BLK == c // TOP)
        ).astype(BF16)
    half = BLK // 2
    if not outer:
        perm[0] = onehot(
            width,
            width,
            lambda r, c: (r // half == (c // (half * TOP)) * TOP + c % TOP)
            & (r % half == (c // TOP) % half),
        ).astype(BF16)
    wide = bz * nz
    lanes[...] = onehot(
        wide,
        wide,
        lambda r, c: (r // nz == (c % nz) // BLK) & (r % nz == (c // nz) * BLK + c % BLK),
    ).astype(BF16)
    near = onehot(
        nz, 2 * nz, lambda r, c: ((c < nz) & (r == c - 1)) | ((c >= nz) & (r == c - nz + 1))
    )
    own = onehot(nz, 2 * nz, lambda r, c: r == c % nz)
    shift[...] = near.astype(BF16)
    shift2[0:nz, :] = near.astype(BF16)
    shift2[nz : 2 * nz, :] = near.astype(BF16)
    dpot[...] = (near - own).astype(BF16)

    @pl.loop(0, tiles)
    def _(o):
        tally[count + o] = 0

    def place(o):
        return o if spread == 1 else lax.rem(o + tiles - me[0], tiles)

    @pl.loop(0, count)
    def _(b):
        o = place(plan[b])
        rank = tally[count + o]
        tally[b] = rank if spread > 1 else o * capacity + rank
        tally[count + o] = rank + 1

    def blank(o, k, ref=None):
        if spread == 1:
            return pltpu.make_async_copy(
                zero, outs[0].at[o * capacity + k], zero_sem.at[o * capacity + k]
            )
        return pltpu.make_async_copy(zero, ref.at[k], zero_sem.at[o * capacity + k])

    def blanks(act):
        if spread == 1:

            @pl.loop(0, tiles)
            def _(o):
                @pl.loop(tally[count + o], capacity)
                def _(k):
                    act(blank(o, k))

            return
        for o in range(tiles):

            @pl.loop(tally[count + o], capacity)
            def _(k, o=o):
                act(blank(o, k, outs[o]))

    blanks(lambda copy: copy.start())

    body = pl.ds(TOP, BLK)

    def scaled(f, v):
        v = v.astype(F32)
        if f == 2:
            return v * 0.5
        return v * lax.rsqrt(jnp.maximum(v, 0.25)) if f == 3 else v

    if not inner:
        for copy in halos:
            copy.wait()
        for plane, ref in zip((0, nx + 1), edges_v):
            for f in range(4):
                fld[f, plane, body, :] = scaled(f, ref[f])
        for ref, dst in zip(edges_v[2:], edges_f):
            for f in range(4):
                dst[f] = scaled(f, ref[f])

    def convert(x, number):
        at = pl.ds(x, number)
        to = pl.ds(x + 1, number)
        fld[0, to, body, :] = c_v[0, at].astype(F32)
        fld[1, to, body, :] = c_v[1, at].astype(F32)
        fld[2, to, body, :] = p_v[at].astype(F32) * 0.5
        d = d_v[at].astype(F32)
        fld[3, to, body, :] = jnp.where(s_v[at] > 0, d * lax.rsqrt(d), 0.0)

    def prepare(i):
        for copy in loads(i):
            copy.wait()
        if not outer:
            convert(i * BLK + m0 - 1, 1)
            convert(i * BLK + m0, 1) if mid else None
            convert(i * BLK + m1 - 1, 1) if mid else None
            convert(i * BLK + m1, 1)

            @pl.loop(0, 4)
            def _(q):
                shifted = q * 4 + (m0 if inner else jnp.where(q >= 2, m1 - m0, 0))
                convert(i * BLK + shifted, 4)

            return

        @pl.loop(0, BLK // 4)
        def _(q):
            x = i * BLK + q * 4
            convert(x, 4)
            for j in range(4):
                for f in range(4):
                    for n, row in enumerate((TOP - 1, TOP + BLK)):
                        fld[f, x + 1 + j, pl.ds(row, 1), :] = edges_f[n][f, pl.ds(x + j, 1), :]

    batch = TOP

    strips = ((0, TOP), (m1, TOP)) if outer else ((m0, m1 - m0),)
    tall = sum(number for _, number in strips)

    def planes(x, number, off=0):
        return [
            jnp.concatenate(
                [
                    fld[f, pl.ds(x + 1, number), pl.ds(TOP + row + off, rows), :]
                    for row, rows in strips
                ],
                axis=1,
            )
            for f in range(4)
        ]

    def update(x):
        m = batch * tall
        c0, c1, pot, s = [v.reshape(m, nz) for v in planes(x, batch)]
        high = s.astype(BF16)
        low = (s - high.astype(F32)).astype(BF16)
        zc = jnp.dot(
            jnp.concatenate([c0, c1], axis=0).astype(BF16),
            shift[...],
            preferred_element_type=F32,
        )
        zs = jnp.dot(
            jnp.concatenate([high, low], axis=1), shift2[...], preferred_element_type=F32
        )
        zp = jnp.dot(pot.astype(BF16), dpot[...], preferred_element_type=F32)

        def plane(j, off=0):
            return [v[0] for v in planes(x + j, 1, off)]

        mid = plane(0)
        below = face(plane(-1), mid)
        charges = []
        for j in range(batch):
            after = plane(j + 1)
            above = face(mid, after)
            total = [above[sp] - below[sp] for sp in range(2)]
            c0, c1, pot, s = mid
            sides = []
            for off in (-1, 1):
                n0, n1, npot, ns = plane(j, off)
                sides.append((n0, n1, npot - pot, ns))
            own = slice(j * tall, (j + 1) * tall)
            again = slice(m + j * tall, m + (j + 1) * tall)
            for part in (slice(0, nz), slice(nz, 2 * nz)):
                sides.append((zc[own, part], zc[again, part], zp[own, part], zs[own, part]))
            sum_a = sum_b = None
            for n0, n1, dp, ns in sides:
                f = s * ns
                h = f * dp
                a = f + h
                b = f - h
                total[0] = total[0] + n0 * a
                total[1] = total[1] + n1 * b
                sum_a = a if sum_a is None else sum_a + a
                sum_b = b if sum_b is None else sum_b + b
            total[0] = total[0] - c0 * sum_b
            total[1] = total[1] - c1 * sum_a
            new = []
            for sp in range(2):
                value = mid[sp] + (ion_step * species_diff[sp]) * total[sp]
                new.append(value.astype(BF16))
                at = 0
                for row, rows in strips:
                    cn_v[sp, x + j, pl.ds(row, rows), :] = new[sp][at : at + rows]
                    at += rows
            charges.append((new[0].astype(F32) - new[1].astype(F32)).astype(BF16)[None])
            mid, below = after, above
        return jnp.concatenate(charges, axis=0)

    def saves(i):
        x = i * BLK
        spots = [(m0, m1 - m0, m0, m1 - m0)]
        if mid:
            spots = [(0, m0, m0, m1 - m0), (m1, TOP, m0, m1 - m0)]
        if outer:
            spots = [(0, BLK, 0, TOP), (0, BLK, m1, TOP)]
        copies = []
        for n, (px, number, row, tall) in enumerate(spots):
            at = (slice(None), pl.ds(x + px, number), pl.ds(row, tall))
            copies.append(pltpu.make_async_copy(cn_v.at[at], cn_hbm.at[at], cn_sem.at[n, i]))
        return copies

    def put(b, n=0):
        return pltpu.make_async_copy(blk.at[b + bz], outs[n].at[tally[b]], blk_sem.at[b])

    def send(b):
        if spread == 1:
            put(b).start()
            return
        shift = place(plan[b])
        for n in range(tiles):

            @pl.when(shift == n)
            def _(n=n):
                put(b, n).start()

    def joined(t, size):
        groups = t.shape[0] // (size * bz)
        return [
            jnp.concatenate(
                [t[(j * bz + m) * size : (j * bz + m + 1) * size] for m in range(bz)], axis=1
            )
            for j in range(groups)
        ]

    offsets = {"inner": (m0, m0 + batch), "mid": (0, m1), "outer": range(0, BLK, batch)}[mode]
    size = BLK if outer else half

    def relayout(i):
        rowsets = []
        for t in range(2 if outer else 1):
            v = jnp.dot(perm[0], chs[t], preferred_element_type=F32).astype(BF16)
            rowsets += joined(v, size)
        res = jnp.dot(
            jnp.concatenate(rowsets, axis=0), lanes[...], preferred_element_type=F32
        ).astype(BF16)
        for k in range(bz):
            for j in range(len(rowsets)):
                blk[(i + 1) * bz + k, :, j * nz : (j + 1) * nz] = res[
                    j * size : (j + 1) * size, k * nz : (k + 1) * nz
                ]

    prepare(0)

    @pl.loop(0, chunks)
    def _(i):
        @pl.when(i + ahead < chunks)
        def _():
            fetch(i + ahead)

        @pl.when(i + 1 < chunks)
        def _():
            prepare(i + 1)

        if inner:
            for copy in rim_loads(i):
                copy.wait()
        relayout(i - 1)
        if inner:
            for n in range(2):
                for half_block in range(2):
                    rim(i, n, half_block)
        for q, offset in enumerate(offsets):
            charge = update(i * BLK + offset)
            m = batch * TOP
            for t in range(2):
                strip = charge[:, t * TOP : (t + 1) * TOP].reshape(m, nz)
                if outer:
                    chs[t, q * m : (q + 1) * m, :] = strip
                else:
                    at = t * half * TOP + q * m
                    chs[0, at : at + m, :] = strip
        for copy in saves(i):
            copy.start()

        @pl.when(i > 0)
        def _():
            for k in range(bz):
                send((i - 1) * bz + k)

    relayout(chunks - 1)
    for k in range(bz):
        send((chunks - 1) * bz + k)

    if inner:
        for copy in halos:
            copy.wait()
        c_x, p_x, d_x, s_x, u_x = raw
        for n, out in enumerate(ends):
            solid = s_x[n] > 0
            out[0] = c_x[n, 0]
            out[1] = c_x[n, 1]
            out[2] = p_x[n]
            out[3] = jnp.where(solid, d_x[n].astype(F32), 0.0).astype(BF16)
            for f in range(3):
                out[4 + f] = jnp.where(solid, u_x[n, f].astype(F32), 0.0).astype(BF16)

    @pl.loop(0, chunks)
    def _(i):
        for copy in saves(i):
            copy.wait()

    @pl.loop(0, count)
    def _(b):
        put(b).wait()

    blanks(lambda copy: copy.wait())


def ion_call(mode, plan, me, c, p, d, s, u, halo, before, capacity, tiles):
    _, nx, ny, nz = c.shape
    count = plan.shape[0]
    chunks = nx // BLK
    bz = nz // BLK
    inner, outer = mode == "inner", mode == "outer"
    args = [plan, me, c, p, d, s] + ([u] if inner else list(halo) + [before])
    deep = BLK if outer else BLK // 2
    wide = BLK * BLK // 2
    spread = tiles if outer else 1
    vm = pltpu.VMEM
    dma = pltpu.SemaphoreType.DMA
    extra = [vm((4, ny, nz), BF16)] * 2
    if inner:
        extra = field_scratch((ny, nz)) + field_scratch((nx, TOP, nz))
        extra += [vm((4, 7, BLK // 2 * TOP, nz), F32), vm((4, BLK // 2 * TOP, nz), jnp.int32)]
        extra.append(dma((2, 5, chunks)))
    if outer:
        extra += [vm((4, nx, nz), BF16)] * 2 + [vm((4, nx, nz), F32)] * 2
    share = 0.5 if outer else 0.25
    part = jax.ShapeDtypeStruct((tiles * capacity // spread, deep, wide), BF16)
    sizes = ((7, ny), (7, ny), (4, nx), (4, nx), (3, nx), (3, nx)) if inner else ()
    ends = [jax.ShapeDtypeStruct((fields, number, nz), BF16) for fields, number in sizes]
    return pl.pallas_call(
        functools.partial(ion_kernel, capacity, mode, spread),
        out_shape=[jax.ShapeDtypeStruct(c.shape, BF16)] + [part] * spread + ends,
        in_specs=[SMEM] * 2 + [HBM] * (len(args) - 2),
        out_specs=[HBM] * (1 + spread) + [VMEM] * len(ends),
        scratch_shapes=[
            vm(c.shape, BF16),
            vm(p.shape, BF16),
            vm(p.shape, BF16),
            vm(p.shape, jnp.int32),
        ]
        + extra
        + [
            vm((4, nx + 2, ROWS, nz), F32),
            vm(c.shape, BF16),
            vm((2 if outer else 1, BLK * TOP, nz), BF16),
            vm((count + bz, deep, wide), BF16),
            vm((deep, wide), BF16),
            vm((1, BLK * TOP, BLK * TOP), BF16),
            vm((bz * nz, bz * nz), BF16),
            vm((nz, 2 * nz), BF16),
            vm((2 * nz, 2 * nz), BF16),
            vm((nz, 2 * nz), BF16),
            pltpu.SMEM((count + tiles,), jnp.int32),
            dma((4, chunks)),
            dma((10,)),
            dma((2, chunks)),
            dma((count,)),
            dma((tiles * capacity,)),
        ],
        input_output_aliases={} if inner else {len(args) - 1: 0},
        compiler_params=pltpu.CompilerParams(vmem_limit_bytes=60 * 2**20),
        cost_estimate=pl.CostEstimate(
            flops=int(100 * p.size * share),
            bytes_accessed=int(60 * p.size * share),
            transcendentals=int(p.size * share),
        ),
    )(*args)


def gather_kernel(boxes, capacity, shifts, aliased, *refs):
    me, parts, refs = refs[0], refs[1 : 1 + len(shifts)], refs[1 + len(shifts) + aliased :]
    out_hbm, sem = refs
    tiles = out_hbm.shape[0] // capacity

    def moves(n):
        base = lax.rem(me[0] + (tiles - shifts[n]), tiles) * capacity
        at = pl.ds(base, parts[n].shape[0])
        copies = []
        for m, ((r0, l0), (x0, y0), rows, width) in enumerate(boxes):
            copies.append(
                pltpu.make_async_copy(
                    parts[n].at[:, pl.ds(r0, rows), pl.ds(l0, width)],
                    out_hbm.at[at, pl.ds(x0, rows), pl.ds(y0, width)],
                    sem.at[n, m],
                )
            )
        return copies

    for n in range(len(shifts)):
        for copy in moves(n):
            copy.start()
    for n in range(len(shifts)):
        for copy in moves(n):
            copy.wait()


def gather_call(mode, me, parts, shifts, before, slots, capacity):
    q, h = BLK * BLK // 4, BLK // 2
    t = TOP
    boxes = {
        "inner": (((0, 0), (t, q), h, 2 * q),),
        "mid": (((0, 0), (0, q), t, 2 * q), ((t, 0), (BLK - t, q), t, 2 * q)),
        "outer": (((0, 0), (0, 0), BLK, q), ((0, q), (0, 3 * q), BLK, q)),
    }[mode]
    args = [me] + list(parts) + ([] if before is None else [before])
    return pl.pallas_call(
        functools.partial(gather_kernel, boxes, capacity, shifts, before is not None),
        out_shape=jax.ShapeDtypeStruct((slots, BLK, BLK * BLK), BF16),
        in_specs=[SMEM]
        + [VMEM] * len(parts)
        + [HBM] * (before is not None),
        out_specs=HBM,
        scratch_shapes=[pltpu.SemaphoreType.DMA((len(parts), len(boxes)))],
        input_output_aliases={} if before is None else {len(args) - 1: 0},
        compiler_params=pltpu.CompilerParams(vmem_limit_bytes=8 * 2**20),
        cost_estimate=pl.CostEstimate(
            flops=0, bytes_accessed=4 * sum(v.size for v in parts), transcendentals=0
        ),
    )(*args)


def flow_kernel(
    u_hbm,
    p_hbm,
    s_hbm,
    cn_hbm,
    xl_hbm,
    xh_hbm,
    yl_hbm,
    yh_hbm,
    ul_hbm,
    uh_hbm,
    un_hbm,
    u_v,
    p_v,
    s_v,
    cn_v,
    uxl_v,
    uxh_v,
    uyl_v,
    uyh_v,
    pxl_v,
    pxh_v,
    pyl_v,
    pyh_v,
    yl_f,
    yh_f,
    fld,
    un_v,
    mix,
    in_sem,
    halo_sem,
    un_sem,
):
    nx, nz = p_hbm.shape[0], p_hbm.shape[2]
    chunks = nx // BLK

    def loads(i):
        part = pl.ds(i * BLK, BLK)
        return (
            pltpu.make_async_copy(u_hbm.at[:, part], u_v.at[:, part], in_sem.at[0, i]),
            pltpu.make_async_copy(p_hbm.at[part], p_v.at[part], in_sem.at[1, i]),
            pltpu.make_async_copy(s_hbm.at[part], s_v.at[part], in_sem.at[2, i]),
            pltpu.make_async_copy(cn_hbm.at[:, part], cn_v.at[:, part], in_sem.at[3, i]),
        )

    pairs = (
        (xl_hbm, uxl_v),
        (xh_hbm, uxh_v),
        (ul_hbm, uyl_v),
        (uh_hbm, uyh_v),
        (xl_hbm, pxl_v),
        (xh_hbm, pxh_v),
        (yl_hbm, pyl_v),
        (yh_hbm, pyh_v),
    )
    halos = [
        pltpu.make_async_copy(
            src.at[2] if n > 3 else (src.at[pl.ds(4, 3)] if n < 2 else src), dst, halo_sem.at[n]
        )
        for n, (src, dst) in enumerate(pairs)
    ]
    for copy in halos:
        copy.start()
    for i in range(min(AHEAD, chunks)):
        for copy in loads(i):
            copy.start()
    for copy in halos:
        copy.wait()
    body = pl.ds(TOP, BLK)
    for plane, ref, pref in ((0, uxl_v, pxl_v), (nx + 1, uxh_v, pxh_v)):
        for f in range(3):
            fld[f, plane, body, :] = ref[f].astype(F32)
        fld[3, plane, body, :] = pref[...].astype(F32)
    for ref, pref, dst in ((uyl_v, pyl_v, yl_f), (uyh_v, pyh_v, yh_f)):
        for f in range(3):
            dst[f] = ref[f].astype(F32)
        dst[3] = pref[...].astype(F32)

    def prepare(i):
        for copy in loads(i):
            copy.wait()

        @pl.loop(0, BLK)
        def _(q):
            x = i * BLK + q
            fluid = s_v[x] > 0
            for f in range(3):
                fld[f, x + 1, body, :] = jnp.where(fluid, u_v[f, x].astype(F32), 0.0)
            fld[3, x + 1, body, :] = p_v[x].astype(F32)
            for f in range(4):
                fld[f, x + 1, pl.ds(TOP - 1, 1), :] = yl_f[f, pl.ds(x, 1), :]
                fld[f, x + 1, pl.ds(TOP + BLK, 1), :] = yh_f[f, pl.ds(x, 1), :]

    up = onehot(nz, nz, lambda r, c: r == c + 1)
    down = onehot(nz, nz, lambda r, c: r == c - 1)
    mix[:, 0:nz] = ((up + down) * viscosity).astype(BF16)
    mix[:, nz : 2 * nz] = ((up - down) * 0.5).astype(BF16)
    batch, tall = 4, 16

    def update(i):
        @pl.loop(0, BLK // batch)
        def _(q):
            x = i * BLK + q * batch
            here = pl.ds(x + 1, batch)
            for y0 in range(0, BLK, tall):
                at = pl.ds(TOP + y0, tall)
                next_y, last_y = pl.ds(TOP + 1 + y0, tall), pl.ds(TOP - 1 + y0, tall)
                own = pl.ds(y0, tall)
                mid = [fld[f, here, at, :] for f in range(4)]
                m = batch * tall
                stack = jnp.concatenate([v.reshape(m, nz) for v in mid], axis=0).astype(BF16)
                z = jnp.dot(stack, mix[...], preferred_element_type=F32)
                z = [z[f * m : (f + 1) * m] for f in range(4)]
                fluid = s_v[pl.ds(x, batch), own, :] > 0
                push = cn_v[0, pl.ds(x, batch), own, :].astype(F32)
                push = (push - cn_v[1, pl.ds(x, batch), own, :].astype(F32)) * 0.5
                plus = [viscosity - 0.5 * u for u in mid[:2]]
                minus = [viscosity + 0.5 * u for u in mid[:2]]
                for a in range(3):
                    total = fld[a, pl.ds(x + 2, batch), at, :] * plus[0]
                    total = total + fld[a, pl.ds(x, batch), at, :] * minus[0]
                    total = total + fld[a, here, next_y, :] * plus[1]
                    total = total + fld[a, here, last_y, :] * minus[1]
                    total = total + z[a][:, :nz].reshape(batch, tall, nz)
                    total = total - mid[2] * z[a][:, nz:].reshape(batch, tall, nz)
                    if a == 0:
                        rise = fld[3, pl.ds(x + 2, batch), at, :] - fld[3, pl.ds(x, batch), at, :]
                    elif a == 1:
                        rise = fld[3, here, next_y, :] - fld[3, here, last_y, :]
                    else:
                        rise = z[3][:, nz:].reshape(batch, tall, nz) * 2.0
                    total = total - push * rise
                    value = mid[a] * (1.0 - 6.0 * viscosity * flow_step) + flow_step * total
                    value = jnp.where(fluid, value, 0.0)
                    un_v[a, pl.ds(x, batch), own, :] = value.astype(BF16)

    def saves(i):
        part = pl.ds(i * BLK, BLK)
        return pltpu.make_async_copy(un_v.at[:, part], un_hbm.at[:, part], un_sem.at[i])

    prepare(0)

    @pl.loop(0, chunks)
    def _(i):
        @pl.when(i + AHEAD < chunks)
        def _():
            for copy in loads(i + AHEAD):
                copy.start()

        @pl.when(i + 1 < chunks)
        def _():
            prepare(i + 1)

        update(i)
        saves(i).start()

    @pl.loop(0, chunks)
    def _(i):
        saves(i).wait()


def flow_call(u, p, s, cn, halo):
    _, nx, ny, nz = u.shape
    chunks = nx // BLK
    vm = pltpu.VMEM
    dma = pltpu.SemaphoreType.DMA
    return pl.pallas_call(
        flow_kernel,
        name="flow",
        out_shape=jax.ShapeDtypeStruct(u.shape, BF16),
        in_specs=[HBM] * 10,
        out_specs=HBM,
        scratch_shapes=[
            vm(u.shape, BF16),
            vm(p.shape, BF16),
            vm(s.shape, jnp.int32),
            vm(cn.shape, BF16),
            vm((3, ny, nz), BF16),
            vm((3, ny, nz), BF16),
            vm((3, nx, nz), BF16),
            vm((3, nx, nz), BF16),
            vm((ny, nz), BF16),
            vm((ny, nz), BF16),
            vm((nx, nz), BF16),
            vm((nx, nz), BF16),
            vm((4, nx, nz), F32),
            vm((4, nx, nz), F32),
            vm((4, nx + 2, ROWS, nz), F32),
            vm(u.shape, BF16),
            vm((nz, 2 * nz), BF16),
            dma((4, chunks)),
            dma((8,)),
            dma((chunks,)),
        ],
        compiler_params=PARAMS,
        cost_estimate=pl.CostEstimate(
            flops=80 * p.size, bytes_accessed=20 * p.size, transcendentals=0
        ),
    )(u, p, s, cn, *halo)


def per_device(concentration, potential, diffusivity, spacer, velocity, balance_plan):
    tiles = lax.axis_size("tile")
    count = balance_plan.shape[0]
    capacity = max(2, (2 * count + tiles - 1) // tiles)
    slots = tiles * capacity

    me = lax.axis_index("tile").astype(jnp.int32)[None]

    def exchange(part):
        part = part.reshape((tiles, capacity) + part.shape[1:])
        part = lax.all_to_all(part, "tile", split_axis=0, concat_axis=0, tiled=True)
        return part.reshape((slots,) + part.shape[2:])

    def pass_on(piece, shift):
        if shift == 0:
            return piece
        return lax.ppermute(piece, "tile", [(i, (i + shift) % tiles) for i in range(tiles)])

    given = (balance_plan[:, 0], me, concentration, potential, diffusivity, spacer, velocity)
    conc, first, *ends = ion_call("inner", *given, None, None, capacity, tiles)
    first = exchange(first)
    x_halo = swap_ends(*ends[:2], "stream")
    y_halo = swap_ends(*ends[2:4], "tile")
    conc, second = ion_call("mid", *given, x_halo, conc, capacity, tiles)
    u_halo = swap_ends(*ends[4:], "tile")
    second = exchange(second)
    halo = x_halo + y_halo
    conc_next, *third = ion_call("outer", *given, halo, conc, capacity, tiles)
    order = sorted(range(1, tiles), key=lambda d: -min(d, tiles - d)) + [0]
    third = [pass_on(third[d], d) for d in order]
    flow_next = flow_call(velocity, potential, spacer, conc_next, halo + u_halo)
    none = jnp.zeros_like(me)
    owned = gather_call("inner", none, [first], (0,), None, slots, capacity)
    owned = gather_call("mid", none, [second], (0,), owned, slots, capacity)
    owned = gather_call("outer", me, third, tuple(order), owned, slots, capacity)
    return conc_next, flow_next, owned


def solution(mesh):
    placed = (
        P(None, "stream", "tile", None),
        P("stream", "tile", None),
        P("stream", "tile", None),
        P("stream", "tile", None),
        P(None, "stream", "tile", None),
        P(("stream", "tile"), None),
    )
    return jax.shard_map(
        per_device,
        mesh=mesh,
        in_specs=placed,
        out_specs=(
            P(None, "stream", "tile", None),
            P(None, "stream", "tile", None),
            P(("stream", "tile"), None, None),
        ),
        check_vma=False,
    )
```
